32 devices in a mesh: groups: 2 (over x), pb: 8 (over z, y), ka: 2 (over core).
Axes of the slice: x: 2, y: 2, z: 4, core: 2. Of those that a mesh axis runs over, the one named last changes fastest.
Arguments:
- queries: bfloat16 [12288, 256], P(('groups', 'pb', 'ka')), parts along dimension 0, may hold values from -6 to 6
- keys: bfloat16 [12288, 256], P(('groups', 'pb', 'ka')), parts along dimension 0, may hold values from -6 to 6
- values: bfloat16 [12288, 256], P(('groups', 'pb', 'ka')), parts along dimension 0, may hold values from -96 to 96
- block_pairs: int32 [4, 8, 16, 9], P('groups', 'pb'), parts along dimension 0, may hold values from -1 to 17, as said below
Outputs:
- attended: bfloat16 [12288, 256], P(('groups', 'pb', 'ka')), parts along dimension 0
The draws below stay inside these ranges and needn't reach their ends.
There are 2 independent parts, one for each index of `groups`. The reference program is written for one: setup_inputs(seed, part) draws one part's arguments, and reference() takes and returns one part's arrays. A program takes and returns all parts, laid end to end along the dimension named above; each array names one. Nothing has to cross between parts.
Inputs may be any that keep to these rules, and one draw needn't show every extreme that they name: Each list block_pairs[h, p, s, :] holds 1 to 9 distinct codes (as defined in the reference program) followed by entries -1; in every draw some list holds 9 codes. Every query block's pair with the key block of the same tokens is kept for every head.
All inputs are finite; a program needn't handle non-finite values.
Results may differ from the reference program's by a relative error of at most 0.0085.
Values may be sent and summed in bfloat16 or wider, within the bound.
A program may use at most 128 MiB of HBM per device.

```python
import jax
import jax.numpy as jnp
from jax import lax

HEAD = 128
HEADS = 2
BLOCK = 128
TOK_DEV = 384
MOST = 9
TOKENS = 6144
N_PB = 8
N_KA = 2


def base_field(key):
    field_shape = (TOKENS, HEADS * HEAD)
    matrix = jax.random.normal(jax.random.fold_in(key, 2), field_shape, jnp.float32)
    return jnp.clip(matrix, -6.0, 6.0)


def draw_queries(key, part):
    matrix = base_field(jax.random.fold_in(key, 11))
    return matrix.astype(jnp.bfloat16)


def draw_keys(key, part):
    matrix = base_field(jax.random.fold_in(key, 12))
    return matrix.astype(jnp.bfloat16)


def draw_block_pairs(key, part):
    shard_count = N_PB * N_KA
    shard_blocks = TOK_DEV // BLOCK
    grid_size = N_KA * shard_blocks * shard_blocks
    levels = jax.random.randint(jax.random.fold_in(key, 21), (HEADS, N_PB, 1, N_KA), 0, 3)
    levels = jnp.broadcast_to(levels, (HEADS, N_PB, N_PB, N_KA)).reshape(HEADS, N_PB, shard_count)
    counts = jax.random.randint(jax.random.fold_in(key, 22), (HEADS, N_PB, shard_count), 1, MOST // 2 + 1)
    counts = counts + levels * (MOST // 4)
    tile_ids = jnp.arange(N_PB)[:, None]
    shard_ids = jnp.arange(shard_count)[None, :]
    own_shard = shard_ids // N_KA == tile_ids
    counts = jnp.where(own_shard[None], jnp.maximum(counts, shard_blocks + 1), counts)
    flat_ids = jnp.arange(N_PB * shard_count).reshape(N_PB, shard_count)
    chosen = jax.random.randint(jax.random.fold_in(key, 23), (HEADS, 1, 1), 0, N_PB * shard_count)
    counts = jnp.minimum(jnp.where(flat_ids[None] == chosen, MOST, counts), MOST)
    places = jnp.arange(grid_size)
    query_local = places // shard_blocks
    key_local = places % shard_blocks
    diagonal = (shard_ids[:, :, None] == tile_ids[:, :, None] * N_KA + (query_local // shard_blocks)[None, None, :]) & (key_local == query_local % shard_blocks)[None, None, :]
    jitter = jax.random.randint(jax.random.fold_in(key, 24), (HEADS, N_PB, shard_count, grid_size), 0, 1 << 16)
    priority = jitter * 1024 + places + diagonal[None].astype(jnp.int32) * (1 << 28)
    ranked = jnp.argsort(-priority, axis=-1, stable=True)[..., :MOST]
    slot_ids = jnp.arange(MOST)
    return jnp.where(slot_ids < counts[..., None], ranked, -1).astype(jnp.int32)


def block_scale(key, extent, split, low, high):
    gain, own = 1.0, jax.random.fold_in(key, 6)
    for dim, blocks in split:
        draws = jnp.exp(jax.random.uniform(jax.random.fold_in(own, dim), (blocks,), jnp.float32, low / len(split), high / len(split)))
        gain = gain * jnp.repeat(draws, extent[dim] // blocks).reshape([-1 if axis == dim else 1 for axis in range(len(extent))])
    return gain


def scatter_about(stream_key, dims, width, reach, cuts=(), kind=jnp.bfloat16):
    result = width * jax.random.normal(stream_key, dims, jnp.float32)
    if cuts:
        result = result * block_scale(stream_key, dims, cuts, -0.22, 0.18)
    return jnp.clip(result, -reach, reach).astype(kind)


def setup_inputs(seed: int = 0, part: int = 0) -> dict:
    splits = jax.random.split(jax.random.key(seed), 5)
    part_splits = jax.random.split(jax.random.fold_in(splits[4], part), 5)
    return {
        "queries": draw_queries(jax.random.fold_in(jax.random.fold_in(splits[4], part), 71), part),
        "keys": draw_keys(jax.random.fold_in(jax.random.fold_in(splits[4], part), 71), part),
        "values": scatter_about(part_splits[2], (TOKENS, HEADS * HEAD), 16.0, 96.0, ((0, 16),)),
        "block_pairs": draw_block_pairs(jax.random.fold_in(jax.random.fold_in(splits[4], part), 71), part),
    }


NEGATIVE_FILL = -1.0e30


def tile_attention(queries, keys, values, block_pairs, head_index, tile_index):
    shard_blocks = TOK_DEV // BLOCK
    tile_rows = N_KA * TOK_DEV
    tile_blocks = N_KA * shard_blocks
    shard_count = N_PB * N_KA
    per_head = lax.dynamic_index_in_dim(block_pairs, head_index, 0, keepdims=False)
    pair_codes = lax.dynamic_index_in_dim(per_head, tile_index, 0, keepdims=False).reshape(-1)
    active = pair_codes >= 0
    clean = jnp.where(active, pair_codes, 0).astype(jnp.int32)
    query_block = (clean // shard_blocks).astype(jnp.int32)
    shard_of = jnp.arange(shard_count * MOST, dtype=jnp.int32) // MOST
    key_block = (shard_of * shard_blocks + clean % shard_blocks).astype(jnp.int32)
    column_start = (head_index * HEAD).astype(jnp.int32)
    row_start = (tile_index * tile_rows).astype(jnp.int32)
    query_tile = lax.dynamic_slice(queries, (row_start, column_start), (tile_rows, HEAD))
    key_cols = lax.dynamic_slice_in_dim(keys, column_start, HEAD, 1).reshape(TOKENS // BLOCK, BLOCK, HEAD)
    value_cols = lax.dynamic_slice_in_dim(values, column_start, HEAD, 1).reshape(TOKENS // BLOCK, BLOCK, HEAD)
    query_sel = query_tile.reshape(tile_blocks, BLOCK, HEAD)[query_block].astype(jnp.float32)
    key_sel = key_cols[key_block].astype(jnp.float32)
    value_sel = value_cols[key_block].astype(jnp.float32)
    scores = jnp.einsum("nqd,nkd->nqk", query_sel, key_sel, precision=lax.Precision.HIGHEST) * (HEAD ** -0.5)
    scores = jnp.where(active[:, None, None], scores, NEGATIVE_FILL)
    slot_max = scores.max(-1)
    is_kept_pair = (query_block[:, None] == jnp.arange(tile_blocks, dtype=jnp.int32)[None, :]) & active[:, None]
    peak = jnp.where(is_kept_pair[:, :, None], slot_max[:, None, :], NEGATIVE_FILL).max(0)
    slot_peak = peak[query_block]
    chances = jnp.where(active[:, None, None], jnp.exp(scores - slot_peak[:, :, None]), 0.0)
    pair_flag = is_kept_pair.astype(jnp.float32)
    total = jnp.einsum("nb,nq->bq", pair_flag, chances.sum(-1), precision=lax.Precision.HIGHEST)
    softmax_weight = lax.optimization_barrier(chances.astype(jnp.bfloat16)).astype(jnp.float32)
    partial_output = jnp.einsum("nqk,nkd->nqd", softmax_weight, value_sel, precision=lax.Precision.HIGHEST)
    running_output = jnp.einsum("vw,vhs->whs", pair_flag, partial_output, precision=lax.Precision.HIGHEST)
    return (running_output / total[:, :, None]).astype(jnp.bfloat16).reshape(tile_rows, HEAD)


def reference(queries, keys, values, block_pairs):
    head_numbers = jnp.repeat(jnp.arange(HEADS, dtype=jnp.int32), N_PB)
    tile_ids = jnp.tile(jnp.arange(N_PB, dtype=jnp.int32), HEADS)

    def one_tile(index_pair):
        return tile_attention(queries, keys, values, block_pairs, index_pair[0], index_pair[1])

    tile_outputs = lax.map(one_tile, (head_numbers, tile_ids))
    tile_outputs = tile_outputs.reshape(HEADS, N_PB, N_KA * TOK_DEV, HEAD).transpose(1, 2, 0, 3)
    return tile_outputs.reshape(TOKENS, HEADS * HEAD)
```

```python
import functools
import math

import jax
import jax.numpy as jnp
from jax import lax
from jax.experimental import pallas as pl
from jax.experimental.pallas import tpu as pltpu
from jax.sharding import PartitionSpec as P

HEAD = 128
BLOCK = 128
STATS = 16
NEGATIVE_FILL = -1e30
EXP2_SCALE = HEAD ** (-0.5) * math.log2(math.e)
MESH = pl.DeviceIdType.MESH


def dot(a, b):
    return lax.dot_general(a, b, (((1,), (0,)), ((), ())), preferred_element_type=jnp.float32)


def kernel(
    n_pb, n_ka, width, cut, q_ref, k_ref, v_ref, pairs_ref, out_ref,
    qbuf, kbuf, vbuf, codes, marks, qturned, vturned, peak, total, accum, osend, orecv, obuf,
    hop_send, query_send, query_recv, code_send, code_recv, side_send, kv_recv,
    swap_send, out_send, out_recv, local_sem,
):
    rows = q_ref.shape[0]
    tile = n_ka * rows
    blocks = rows // BLOCK
    n_y = width
    n_z = n_pb // n_y
    core = lax.axis_index("ka")
    place = lax.axis_index("pb")
    z, y = place // n_y, place % n_y
    other = 1 - core
    far_y = 1 - y
    across = z * n_y + far_y
    has_left, has_right = z > 0, z < n_z - 1
    piece = rows // cut

    barrier = pltpu.get_barrier_semaphore()

    def greet(pb, ka):
        pl.semaphore_signal(barrier, inc=1, device_id={"pb": pb, "ka": ka}, device_id_type=MESH)

    def others(act):
        for step in range(1, n_z):
            act(lax.rem(z + step, n_z))

    for ka in range(n_ka):
        others(lambda layer, ka=ka: greet(layer * n_y + y, ka))
        greet(across, ka)
    greet(place, other)

    def columns(head):
        return pl.ds(pl.multiple_of(head * HEAD, HEAD), HEAD)

    def rows_of(ka):
        return pl.ds(pl.multiple_of(ka * rows, BLOCK), rows)

    my_rows, other_rows = rows_of(core), rows_of(other)

    stage = [
        pltpu.make_async_copy(k_ref.at[:, columns(core)], kbuf.at[y, my_rows], local_sem.at[0]),
        pltpu.make_async_copy(q_ref.at[:, columns(core)], qbuf.at[z, my_rows], local_sem.at[1]),
        pltpu.make_async_copy(v_ref.at[:, columns(core)], vbuf.at[y, my_rows], local_sem.at[2]),
    ]
    for item in stage:
        item.start()

    def remote(source, target, send_sem, recv_sem, **device):
        return pltpu.make_async_remote_copy(
            src_ref=source, dst_ref=target, send_sem=send_sem, recv_sem=recv_sem,
            device_id=device, device_id_type=MESH,
        )

    block_of_row = lax.broadcasted_iota(jnp.int32, (tile, HEAD), 0) // BLOCK
    lane = lax.broadcasted_iota(jnp.int32, (tile, HEAD), 1)
    for side in range(n_y):
        here = lane == block_of_row + side * n_ka * blocks
        marks[side] = jnp.where(here, 1.0, 0.0).astype(marks.dtype)
    pad = qturned.shape[1] - HEAD - STATS
    for layer in range(n_z):
        qturned[layer, pl.ds(HEAD + STATS, pad), :] = jnp.zeros((pad, tile), qturned.dtype)

    pl.semaphore_wait(barrier, n_ka * n_z + 1)

    def query_part(layer, ka, part):
        return qbuf.at[layer, pl.ds(pl.multiple_of(ka * rows + part * piece, 16), piece)]

    def hop(way, head, part):
        return remote(
            q_ref.at[pl.ds(part * piece, piece), columns(head)], query_part(z, core, part),
            hop_send.at[way, head, part], query_recv.at[z, core, part],
            pb=place + (n_y if way else -n_y), ka=head,
        )

    def hops(act):
        for part in range(cut):
            for way, there in ((0, has_left), (1, has_right)):
                @pl.when(there)
                def _():
                    for head in range(n_ka):
                        act(hop(way, head, part))

    def side_copy(which, head):
        source, target = ((k_ref, kbuf), (v_ref, vbuf))[which]
        return remote(
            source.at[:, columns(head)], target.at[y, my_rows],
            side_send.at[which, head], kv_recv.at[which, y, core], pb=across, ka=head,
        )

    def swap(which):
        source, target = (
            (k_ref, kbuf.at[y, my_rows]), (v_ref, vbuf.at[y, my_rows]), (q_ref, qbuf.at[z, my_rows]),
        )[which]
        recv = query_recv.at[z, core, 0] if which == 2 else kv_recv.at[which, y, core]
        return remote(
            source.at[:, columns(other)], target, swap_send.at[which], recv, ka=other,
        )

    def code_copy(layer):
        return remote(
            pairs_ref.at[core], codes.at[z], code_send.at[layer], code_recv.at[z],
            pb=layer * n_y + y,
        )

    hops(lambda item: item.start())
    for which in range(2):
        for head in range(n_ka):
            side_copy(which, head).start()
    for which in (0, 2, 1):
        swap(which).start()
    others(lambda layer: code_copy(layer).start())

    def wait_kv(which, side, ka):
        target = (kbuf, vbuf)[which].at[side, rows_of(ka)]
        remote(target, target, side_send.at[which, 0], kv_recv.at[which, side, ka], ka=other).wait_recv()

    row = lax.broadcasted_iota(jnp.int32, (STATS, tile), 0)
    shards = pairs_ref.shape[3]
    pick = (
        lax.broadcasted_iota(jnp.int32, (STATS, shards), 1)
        == lax.broadcasted_iota(jnp.int32, (STATS, shards), 0) // blocks + z * n_y * n_ka
    )
    pick = jnp.where(pick, 1.0, 0.0).astype(jnp.bfloat16)
    wanted = lax.broadcasted_iota(jnp.int32, (STATS, tile), 1) // BLOCK * blocks + row % blocks
    wanted = wanted.astype(jnp.float32)

    def prepare(layer, listed):
        spread = lax.dot_general(
            pick, listed.astype(jnp.float32).astype(jnp.bfloat16), (((1,), (1,)), ((), ())),
            preferred_element_type=jnp.float32,
        )
        hit = None
        for slot in range(listed.shape[0]):
            same = jnp.broadcast_to(spread[:, slot : slot + 1], (STATS, tile)) == wanted
            hit = same if hit is None else hit | same
        qturned[layer, pl.ds(HEAD, STATS), :] = jnp.where(hit, 0.0, NEGATIVE_FILL).astype(qturned.dtype)
        qturned[layer, pl.ds(0, HEAD), :] = qbuf[layer].T

    def scores_of(layer, ka, side):
        keys = jnp.concatenate([kbuf[side], marks[side]], axis=1)
        return dot(keys, qturned[layer, :, pl.ds(ka * rows, rows)])

    def first_half(layer):
        for ka in range(n_ka):
            span = pl.ds(ka * rows, rows)
            scores = scores_of(layer, ka, y)
            top = scores.max(0, keepdims=True)
            chances = jnp.exp2((scores - top) * EXP2_SCALE)
            peak[layer, :, span] = top
            total[layer, :, span] = chances.sum(0, keepdims=True)
            accum[layer, :, span] = dot(vturned[y], chances.astype(jnp.bfloat16))

    stat_row = lax.broadcasted_iota(jnp.int32, (STATS, rows), 0)

    def second_half(layer, ka):
        span = pl.ds(ka * rows, rows)
        scores = scores_of(layer, ka, far_y)
        before = peak[layer, :, span]
        top = jnp.maximum(before, scores.max(0, keepdims=True))
        rescale = jnp.exp2((before - top) * EXP2_SCALE)
        chances = jnp.exp2((scores - top) * EXP2_SCALE)
        whole = total[layer, :, span] * rescale + chances.sum(0, keepdims=True)
        mixed = accum[layer, :, span] * rescale + dot(vturned[far_y], chances.astype(jnp.bfloat16))
        osend[layer, ka, pl.ds(0, HEAD), :] = (mixed * (1.0 / whole)).astype(osend.dtype)
        level = top * EXP2_SCALE + jnp.log2(whole)
        high = level.astype(jnp.bfloat16).astype(jnp.float32)
        middle = (level - high).astype(jnp.bfloat16).astype(jnp.float32)
        low = level - high - middle
        stats = jnp.where(stat_row == 0, high, jnp.where(stat_row == 1, middle, jnp.where(stat_row == 2, low, 0.0)))
        osend[layer, ka, pl.ds(HEAD, STATS), :] = stats.astype(osend.dtype)

    def give(layer, ka):
        return remote(
            osend.at[layer, ka], orecv.at[z, core], out_send.at[layer, ka], out_recv.at[z, core],
            pb=layer * n_y + y, ka=ka,
        )

    def give_other():
        return remote(
            osend.at[z, other], orecv.at[z, core], out_send.at[z, other], out_recv.at[z, core], ka=other,
        )

    shorter = jnp.minimum(z, n_z - 1 - z)

    def layer_at(turn):
        both = turn <= 2 * shorter
        away = jnp.where(both, (turn + 1) // 2, turn - shorter)
        right = jnp.where(both, turn % 2 == 1, z < n_z - 1 - z)
        return jnp.where(right, z + away, z - away)

    def onward(layer):
        return jnp.logical_or(
            jnp.logical_and(layer < z, has_right), jnp.logical_and(layer > z, has_left)
        )

    def forward(layer, ka, part):
        ref = query_part(layer, ka, part)
        return remote(
            ref, ref, query_send.at[layer, ka, part], query_recv.at[layer, ka, part],
            pb=jnp.where(layer < z, place + n_y, place - n_y),
        )

    def take(layer):
        for part in range(cut):
            for ka in range(n_ka):
                ref = query_part(layer, ka, part)
                remote(
                    ref, ref, query_send.at[layer, ka, part], query_recv.at[layer, ka, part], ka=other
                ).wait_recv()

                @pl.when(onward(layer))
                def _():
                    forward(layer, ka, part).start()

    def ready(layer):
        code_copy_in = remote(codes.at[layer], codes.at[layer], code_send.at[layer], code_recv.at[layer], ka=other)
        code_copy_in.wait_recv()
        prepare(layer, codes[layer, :, 0, :])

    def finish(layer):
        for ka in range(n_ka):
            second_half(layer, ka)
            give(layer, ka).start()

    for item in stage:
        item.wait()
    wait_kv(0, y, other)
    incoming = qbuf.at[z, other_rows]
    remote(incoming, incoming, swap_send.at[2], query_recv.at[z, other, 0], ka=other).wait_recv()
    prepare(z, pairs_ref[core, :, 0, :])
    wait_kv(1, y, other)
    vturned[y] = vbuf[y].T
    first_half(z)

    soon = min(3, n_z)
    for turn in range(1, soon):
        layer = layer_at(turn)
        take(layer)
        ready(layer)
        first_half(layer)

    if n_z > 3:
        third = layer_at(3)

        @pl.when(onward(third))
        def _():
            take(third)

    for which in range(2):
        for ka in range(n_ka):
            wait_kv(which, far_y, ka)
    vturned[far_y] = vbuf[far_y].T
    for turn in range(1, soon):
        finish(layer_at(turn))

    def visit(turn, carry):
        layer = layer_at(turn)

        @pl.when(jnp.logical_or(turn != 3, jnp.logical_not(onward(layer))))
        def _():
            take(layer)

        ready(layer)
        first_half(layer)
        finish(layer)
        return carry

    lax.fori_loop(3, n_z, visit, 0)

    for ka in range(n_ka):
        second_half(z, ka)
    give_other().start()

    def part_of(head, layer, local):
        ref = osend.at[z, core] if local else orecv.at[layer, head]
        stats = ref[pl.ds(HEAD, STATS), :].astype(jnp.float32)
        return ref, stats[0:1] + stats[1:2] + stats[2:3]

    def wait_out(layer, head):
        ref = orecv.at[layer, head]
        remote(ref, ref, out_send.at[z, 0], out_recv.at[layer, head], ka=other).wait_recv()

    for turn in range(1, n_z):
        for head in range(n_ka):
            wait_out(layer_at(turn), head)
    wait_out(z, other)

    keeps = []
    for index, head in enumerate((core, other)):
        parts = [part_of(head, z, index == 0)]
        parts += [part_of(head, layer_at(turn), False) for turn in range(1, n_z)]
        top = functools.reduce(jnp.maximum, [level for _, level in parts])
        shares = [jnp.exp2(level - top) for _, level in parts]
        scale = 1.0 / functools.reduce(jnp.add, shares)
        mixed = None
        for (ref, _), share in zip(parts, shares):
            term = ref[pl.ds(0, HEAD), :].astype(jnp.float32) * (share * scale)
            mixed = term if mixed is None else mixed + term
        obuf[index] = mixed.T.astype(obuf.dtype)
        keep = pltpu.make_async_copy(obuf.at[index], out_ref.at[:, columns(head)], local_sem.at[3 + index])
        keep.start()
        keeps.append(keep)

    hops(lambda item: item.wait_send())
    for which in range(2):
        for head in range(n_ka):
            side_copy(which, head).wait_send()
    for which in range(3):
        swap(which).wait_send()
    others(lambda layer: code_copy(layer).wait_send())

    def drain(turn, carry):
        layer = layer_at(turn)
        for ka in range(n_ka):
            give(layer, ka).wait_send()

        @pl.when(onward(layer))
        def _():
            for ka in range(n_ka):
                for part in range(cut):
                    forward(layer, ka, part).wait_send()
        return carry

    lax.fori_loop(1, n_z, drain, 0)
    give_other().wait_send()
    for keep in keeps:
        keep.wait()


def solution(mesh):
    n_pb, n_ka = mesh.shape["pb"], mesh.shape["ka"]
    width = 2
    cut = 2

    def local(queries, keys, values, block_pairs):
        rows = queries.shape[0]
        tile = n_ka * rows
        shards, most = block_pairs.shape[2:]
        n_z = n_pb // width
        anywhere = pl.BlockSpec(memory_space=pl.ANY)
        half = jnp.bfloat16
        dma = pltpu.SemaphoreType.DMA
        return pl.pallas_call(
            functools.partial(kernel, n_pb, n_ka, width, cut),
            out_shape=jax.ShapeDtypeStruct(queries.shape, queries.dtype),
            in_specs=[anywhere, anywhere, anywhere, pl.BlockSpec(memory_space=pltpu.VMEM)],
            out_specs=anywhere,
            scratch_shapes=[
                pltpu.VMEM((n_z, tile, HEAD), half),
                pltpu.VMEM((width, tile, HEAD), half),
                pltpu.VMEM((width, tile, HEAD), half),
                pltpu.VMEM((n_z, most, 1, shards), jnp.int32),
                pltpu.VMEM((width, tile, HEAD), half),
                pltpu.VMEM((n_z, 2 * HEAD, tile), half),
                pltpu.VMEM((width, HEAD, tile), half),
                pltpu.VMEM((n_z, 1, tile), jnp.float32),
                pltpu.VMEM((n_z, 1, tile), jnp.float32),
                pltpu.VMEM((n_z, HEAD, tile), jnp.float32),
                pltpu.VMEM((n_z, n_ka, HEAD + STATS, rows), half),
                pltpu.VMEM((n_z, n_ka, HEAD + STATS, rows), half),
                pltpu.VMEM((n_ka, rows, HEAD), half),
                dma((2, n_ka, cut)),
                dma((n_z, n_ka, cut)),
                dma((n_z, n_ka, cut)),
                dma((n_z,)),
                dma((n_z,)),
                dma((2, n_ka)),
                dma((2, width, n_ka)),
                dma((3,)),
                dma((n_z, n_ka)),
                dma((n_z, n_ka)),
                dma((5,)),
            ],
            compiler_params=pltpu.CompilerParams(
                collective_id=0, has_side_effects=True, vmem_limit_bytes=56 * 1024 * 1024
            ),
        )(queries, keys, values, block_pairs.transpose(0, 3, 1, 2))

    rows_spec = P(("groups", "pb", "ka"), None)
    return jax.shard_map(
        local, mesh=mesh,
        in_specs=(rows_spec, rows_spec, rows_spec, P("groups", "pb", None, None)),
        out_specs=rows_spec, check_vma=False,
    )
```

```python
import functools
import math

import jax
import jax.numpy as jnp
from jax import lax
from jax.experimental import pallas as pl
from jax.experimental.pallas import tpu as pltpu
from jax.sharding import PartitionSpec as P

HEAD = 128
HEADS = 2
BLOCK = 128
NEGATIVE_FILL = -1e30
EXP2_SCALE = HEAD ** (-0.5) * math.log2(math.e)
MESH = pl.DeviceIdType.MESH
LEFT, RIGHT, ACROSS = 0, 1, 2
STATS = 16


def kernel(
    n_pb, n_ka, width, q_ref, k_ref, v_ref, pairs_ref, out_ref,
    qbuf, kbuf, vbuf, bias, peak, total, accum, obuf, qturned, qhelp, codes, ohelp, ogiven,
    send_sem, recv_sem, local_sem, swap_send, swap_recv, help_send, help_recv,
):
    rows = q_ref.shape[0]
    tile = n_ka * rows
    late = BLOCK - BLOCK // 4
    half = (rows - late) // 2
    n_y = width
    n_z = n_pb // n_y
    core = lax.axis_index("ka")
    place = lax.axis_index("pb")
    z, y = place // n_y, place % n_y
    other = 1 - core
    across = z * n_y + (1 - y)
    has_left, has_right = z > 0, z < n_z - 1
    at_end = jnp.logical_not(jnp.logical_and(has_left, has_right))
    aided = n_z > 3
    by_left, by_right = z == 1, z == n_z - 2
    helps = jnp.logical_or(by_left, by_right)
    targets = {LEFT: place - n_y, RIGHT: place + n_y, ACROSS: across}

    barrier = pltpu.get_barrier_semaphore()
    pl.semaphore_signal(barrier, inc=1, device_id={"ka": other}, device_id_type=MESH)
    pl.semaphore_signal(barrier, inc=1, device_id={"pb": across}, device_id_type=MESH)

    @pl.when(has_left)
    def _():
        pl.semaphore_signal(barrier, inc=1, device_id={"pb": place - n_y}, device_id_type=MESH)

    @pl.when(has_right)
    def _():
        pl.semaphore_signal(barrier, inc=1, device_id={"pb": place + n_y}, device_id_type=MESH)

    my_columns = pl.ds(pl.multiple_of(core * HEAD, HEAD), HEAD)
    other_columns = pl.ds(pl.multiple_of(other * HEAD, HEAD), HEAD)
    my_rows = pl.ds(pl.multiple_of(core * rows, BLOCK), rows)
    other_rows = pl.ds(pl.multiple_of(other * rows, BLOCK), rows)

    stage = [
        pltpu.make_async_copy(k_ref.at[:, my_columns], kbuf.at[place, my_rows], local_sem.at[0]),
        pltpu.make_async_copy(v_ref.at[:, my_columns], vbuf.at[place, my_rows], local_sem.at[1]),
        pltpu.make_async_copy(q_ref.at[:, my_columns], qbuf.at[my_rows], local_sem.at[2]),
    ]
    for item in stage:
        item.start()

    pl.semaphore_wait(
        barrier, 2 + has_left.astype(jnp.int32) + has_right.astype(jnp.int32)
    )

    def swap(index, source, target):
        return pltpu.make_async_remote_copy(
            src_ref=source, dst_ref=target, send_sem=swap_send.at[index],
            recv_sem=swap_recv.at[index], device_id={"ka": other}, device_id_type=MESH,
        )

    swaps_out = [
        swap(0, k_ref.at[:, other_columns], kbuf.at[place, my_rows]),
        swap(1, v_ref.at[:, other_columns], vbuf.at[place, my_rows]),
        swap(2, q_ref.at[:, other_columns], qbuf.at[my_rows]),
    ]
    for item in swaps_out:
        item.start()

    spans = ((0, rows), (0, half), (half, half), (2 * half, late))
    early, last = (0, 1, 2), 3

    def part(p, a, m):
        start, size = spans[m]
        span = pl.ds(pl.multiple_of(a * rows + start, 16), size)
        return (vbuf if m else kbuf).at[p, span]

    def message(way, p, a, m, source=None):
        ref = part(p, a, m)
        return pltpu.make_async_remote_copy(
            src_ref=ref if source is None else source, dst_ref=ref, send_sem=send_sem.at[way, p, a, m],
            recv_sem=recv_sem.at[p, a, m], device_id={"pb": targets[way]}, device_id_type=MESH,
        )

    def send(way, p, a, m, source=None):
        if way == ACROSS:
            message(way, p, a, m, source).start()
        else:
            @pl.when(has_left if way == LEFT else has_right)
            def _():
                message(way, p, a, m, source).start()

    def arrive(p, a, m):
        message(ACROSS, p, a, m).wait_recv()

    def send_own(a, parts, source=None, ways=(ACROSS, LEFT, RIGHT)):
        for m in parts:
            start, size = spans[m]
            view = None if source is None else source.at[pl.ds(start, size), my_columns]
            for way in ways:
                send(way, place, a, m, view)

    send_own(core, (0,), k_ref)
    send_own(core, (last,), v_ref, (ACROSS,))
    send_own(core, (1, 2), v_ref)

    swap(0, k_ref.at[:, other_columns], kbuf.at[place, other_rows]).wait_recv()
    send_own(other, (0,))
    swap(1, v_ref.at[:, other_columns], vbuf.at[place, other_rows]).wait_recv()
    send_own(other, (last,), None, (ACROSS,))
    send_own(other, (1, 2))
    send_own(core, (last,), v_ref, (LEFT, RIGHT))
    send_own(other, (last,), None, (LEFT, RIGHT))

    helper = jnp.where(has_left, place - n_y, place + n_y)
    client = jnp.where(by_left, place - n_y, place + n_y)

    def ask(which):
        source, target = ((qbuf, qhelp), (pairs_ref.at[core], codes))[which]
        return pltpu.make_async_remote_copy(
            src_ref=source, dst_ref=target, send_sem=help_send.at[which],
            recv_sem=help_recv.at[which], device_id={"pb": helper}, device_id_type=MESH,
        )

    answer = pltpu.make_async_remote_copy(
        src_ref=ogiven, dst_ref=ohelp, send_sem=help_send.at[2],
        recv_sem=help_recv.at[2], device_id={"pb": client}, device_id_type=MESH,
    )

    blocks = rows // BLOCK

    def mark(slot, listed):
        listed = listed.T
        shards = listed.shape[0]
        query_block = lax.broadcasted_iota(jnp.int32, (shards, tile), 1) // BLOCK
        kept = [None] * blocks
        for code in range(listed.shape[1]):
            column = jnp.broadcast_to(listed[:, code : code + 1], (shards, tile))
            for j in range(blocks):
                hit = column == query_block * blocks + j
                kept[j] = hit if kept[j] is None else kept[j] | hit
        for j in range(blocks):
            bias[slot, j] = jnp.where(kept[j], 0.0, NEGATIVE_FILL).astype(jnp.float32)

    for item in stage:
        item.wait()
    swap(2, q_ref.at[:, other_columns], qbuf.at[other_rows]).wait_recv()

    if aided:
        @pl.when(at_end)
        def _():
            for which in range(2):
                ask(which).start()

    mark(0, pairs_ref[core, :, 0, :])
    peak[...] = jnp.full_like(peak, NEGATIVE_FILL)
    total[...] = jnp.zeros_like(total)
    accum[...] = jnp.zeros_like(accum)
    qturned[0] = qbuf[...].T

    def attend(p, slot=0):
        turned = vbuf[p].T
        scores = lax.dot_general(
            kbuf[p], qturned[slot], (((1,), (0,)), ((), ())),
            preferred_element_type=jnp.float32,
        )
        masked = []
        for a in range(n_ka):
            for j in range(blocks):
                row = (a * blocks + j) * BLOCK
                line = bias[slot, j, pl.ds(p * n_ka + a, 1), :]
                masked.append(scores[row : row + BLOCK] + line)
        scores = jnp.concatenate(masked, axis=0)
        before = peak[slot]
        after = jnp.maximum(before, scores.max(0, keepdims=True))
        rescale = jnp.exp2((before - after) * EXP2_SCALE)
        chances = jnp.exp2((scores - after) * EXP2_SCALE)
        peak[slot] = after
        total[slot] = total[slot] * rescale + chances.sum(0, keepdims=True)
        accum[slot] = accum[slot] * rescale + lax.dot_general(
            turned, chances.astype(jnp.bfloat16), (((1,), (0,)), ((), ())),
            preferred_element_type=jnp.float32,
        )

    attend(place)

    for a in (core, other):
        arrive(across, a, last)
        send(LEFT, across, a, last)
        send(RIGHT, across, a, last)

    def sides(step):
        left, right = z - step >= 0, z + step < n_z
        if aided:
            spared = jnp.logical_and(at_end, step == 2)
            left = jnp.logical_and(left, jnp.logical_not(spared))
            right = jnp.logical_and(right, jnp.logical_not(spared))
        return ((z - step, left, RIGHT), (z + step, right, LEFT))

    def onward(step, way, p, a, m):
        if aided:
            stops = jnp.logical_and(step == 1, by_left if way == LEFT else by_right)

            @pl.when(jnp.logical_not(stops))
            def _():
                send(way, p, a, m)
        else:
            send(way, p, a, m)

    def aside(step, far, p, a, m):
        if aided:
            direct = jnp.logical_and(step == 1, jnp.logical_or(far == 0, far == n_z - 1))

            @pl.when(jnp.logical_not(direct))
            def _():
                send(ACROSS, p, a, m)
        else:
            send(ACROSS, p, a, m)

    def attend_across(p):
        for a in (core, other):
            for m in early:
                arrive(p, a, m)
        attend(p)

    def forward_early(step):
        for a in (core, other):
            for m in early:
                if aided and isinstance(step, int) and step == 1:
                    @pl.when(at_end)
                    def _(a=a, m=m):
                        arrive(across, a, m)
                        send(LEFT, across, a, m)
                        send(RIGHT, across, a, m)

                for far, valid, way in sides(step):
                    @pl.when(valid)
                    def _(far=far, way=way):
                        p = far * n_y + y
                        arrive(p, a, m)
                        onward(step, way, p, a, m)
                        aside(step, far, p, a, m)

    def forward_last(step):
        for a in (core, other):
            for far, valid, way in sides(step):
                @pl.when(valid)
                def _(far=far, way=way):
                    for near in (y, 1 - y):
                        p = far * n_y + near
                        arrive(p, a, last)
                        onward(step, way, p, a, last)

    def across_sides(step):
        for far, valid, way in sides(step):
            @pl.when(valid)
            def _(far=far, way=way):
                p = far * n_y + 1 - y
                if aided:
                    had = jnp.logical_and(step == 1, by_left if way == LEFT else by_right)

                    @pl.when(jnp.logical_not(had))
                    def _():
                        for a in (core, other):
                            for m in early:
                                arrive(p, a, m)
                    attend(p)
                else:
                    attend_across(p)

    def near_sides(step):
        for far, valid, _ in sides(step):
            @pl.when(valid)
            def _(far=far):
                attend(far * n_y + y)

    forward_early(1)
    forward_last(1)
    if aided:
        @pl.when(jnp.logical_not(at_end))
        def _():
            for a in (core, other):
                for m in early:
                    arrive(across, a, m)

        attend(across)

        @pl.when(helps)
        def _():
            for which in range(2):
                ask(which).wait_recv()
            mark(1, codes[:, 0, :])
            qturned[1] = qhelp[...].T
            behind = jnp.where(by_left, z + 1, z - 1) * n_y
            attend(behind + y, 1)
            for a in (core, other):
                for m in early:
                    arrive(behind + 1 - y, a, m)
            attend(behind + 1 - y, 1)
            whole = total[1]
            ogiven[pl.ds(0, HEAD), :] = (accum[1] * (1.0 / whole)).astype(ogiven.dtype)
            level = peak[1] * EXP2_SCALE + jnp.log2(whole)
            high = level.astype(jnp.bfloat16).astype(jnp.float32)
            middle = (level - high).astype(jnp.bfloat16).astype(jnp.float32)
            low = level - high - middle
            row = lax.broadcasted_iota(jnp.int32, (STATS, tile), 0)
            stats = jnp.where(row == 0, high, jnp.where(row == 1, middle, jnp.where(row == 2, low, 0.0)))
            ogiven[pl.ds(HEAD, STATS), :] = stats.astype(ogiven.dtype)
            answer.start()
    else:
        attend_across(across)

    def one_step(step, carry):
        @pl.when(at_end)
        def _():
            near_sides(step)

        @pl.when(step < n_z - 1)
        def _():
            forward_early(step + 1)

        @pl.when(at_end)
        def _():
            across_sides(step)

        @pl.when(step < n_z - 1)
        def _():
            forward_last(step + 1)

        @pl.when(jnp.logical_not(at_end))
        def _():
            near_sides(step)
            across_sides(step)
        return carry

    lax.fori_loop(1, n_z, one_step, 0)

    if aided:
        @pl.when(at_end)
        def _():
            answer.wait_recv()
            stats = ohelp[pl.ds(HEAD, STATS), :].astype(jnp.float32)
            level = stats[0:1] + stats[1:2] + stats[2:3]
            before = peak[0] * EXP2_SCALE
            after = jnp.maximum(before, level)
            rescale, share = jnp.exp2(before - after), jnp.exp2(level - after)
            total[0] = total[0] * rescale + share
            accum[0] = accum[0] * rescale + ohelp[pl.ds(0, HEAD), :].astype(jnp.float32) * share

    def finish(which):
        span = pl.ds(pl.multiple_of(which * rows, BLOCK), rows)
        done = accum[0, :, span] / total[0, :, span]
        obuf[span, :] = done.T.astype(obuf.dtype)

    finish(other)
    give = pltpu.make_async_remote_copy(
        src_ref=obuf.at[other_rows], dst_ref=out_ref.at[:, my_columns],
        send_sem=swap_send.at[3], recv_sem=swap_recv.at[3],
        device_id={"ka": other}, device_id_type=MESH,
    )
    give.start()
    finish(core)
    keep = pltpu.make_async_copy(obuf.at[my_rows], out_ref.at[:, my_columns], local_sem.at[3])
    keep.start()

    def drain(way, far, near, a, m):
        message(way, far * n_y + near, a, m).wait_send()

    def drain_line(way):
        def body(far, carry):
            stops = jnp.logical_and(by_left, far == 2) if way == LEFT else jnp.logical_and(by_right, far == n_z - 3)

            @pl.when(jnp.logical_not(jnp.logical_and(stops, aided)))
            def _():
                for a in range(n_ka):
                    for m in early:
                        drain(way, far, y, a, m)
                    for near in range(n_y):
                        drain(way, far, near, a, last)

            return carry
        return body

    lax.fori_loop(jnp.where(has_left, z, n_z), n_z, drain_line(LEFT), 0)
    lax.fori_loop(0, jnp.where(has_right, z + 1, 0), drain_line(RIGHT), 0)

    def drain_across(far, carry):
        if aided:
            beside = jnp.logical_or(far == z + 1, far == z - 1)
            direct = jnp.logical_and(beside, jnp.logical_or(far == 0, far == n_z - 1))
            spared = jnp.logical_and(at_end, jnp.logical_or(far == z + 2, far == z - 2))
            unsent = jnp.logical_or(direct, spared)
        else:
            unsent = far < 0

        @pl.when(jnp.logical_not(unsent))
        def _():
            for a in range(n_ka):
                for m in early:
                    drain(ACROSS, far, y, a, m)

        return carry

    lax.fori_loop(0, n_z, drain_across, 0)
    for a in range(n_ka):
        drain(ACROSS, z, y, a, last)
    if aided:
        for way, here in ((RIGHT, z == 0), (LEFT, z == n_z - 1)):
            @pl.when(here)
            def _(way=way):
                for a in range(n_ka):
                    for m in early:
                        drain(way, z, 1 - y, a, m)
                for which in range(2):
                    ask(which).wait_send()

        @pl.when(helps)
        def _():
            answer.wait_send()
    for item in swaps_out:
        item.wait_send()
    give.wait_send()
    keep.wait()
    pltpu.make_async_remote_copy(
        src_ref=obuf.at[other_rows], dst_ref=out_ref.at[:, other_columns],
        send_sem=swap_send.at[3], recv_sem=swap_recv.at[3],
        device_id={"ka": other}, device_id_type=MESH,
    ).wait_recv()


def solution(mesh):
    n_pb, n_ka = mesh.shape["pb"], mesh.shape["ka"]
    width = 2

    def local(queries, keys, values, block_pairs):
        rows = queries.shape[0]
        tile = n_ka * rows
        shards = block_pairs.shape[2]
        anywhere = pl.BlockSpec(memory_space=pl.ANY)
        return pl.pallas_call(
            functools.partial(kernel, n_pb, n_ka, width),
            out_shape=jax.ShapeDtypeStruct(queries.shape, queries.dtype),
            in_specs=[anywhere, anywhere, anywhere, pl.BlockSpec(memory_space=pltpu.VMEM)],
            out_specs=anywhere,
            scratch_shapes=[
                pltpu.VMEM((tile, HEAD), jnp.bfloat16),
                pltpu.VMEM((n_pb, tile, HEAD), jnp.bfloat16),
                pltpu.VMEM((n_pb, tile, HEAD), jnp.bfloat16),
                pltpu.VMEM((2, rows // BLOCK, shards, tile), jnp.float32),
                pltpu.VMEM((2, 1, tile), jnp.float32),
                pltpu.VMEM((2, 1, tile), jnp.float32),
                pltpu.VMEM((2, HEAD, tile), jnp.float32),
                pltpu.VMEM((tile, HEAD), jnp.bfloat16),
                pltpu.VMEM((2, HEAD, tile), jnp.bfloat16),
                pltpu.VMEM((tile, HEAD), jnp.bfloat16),
                pltpu.VMEM((block_pairs.shape[3], 1, shards), jnp.int32),
                pltpu.VMEM((HEAD + STATS, tile), jnp.bfloat16),
                pltpu.VMEM((HEAD + STATS, tile), jnp.bfloat16),
                pltpu.SemaphoreType.DMA((3, n_pb, n_ka, 4)),
                pltpu.SemaphoreType.DMA((n_pb, n_ka, 4)),
                pltpu.SemaphoreType.DMA((4,)),
                pltpu.SemaphoreType.DMA((4,)),
                pltpu.SemaphoreType.DMA((4,)),
                pltpu.SemaphoreType.DMA((3,)),
                pltpu.SemaphoreType.DMA((3,)),
            ],
            compiler_params=pltpu.CompilerParams(collective_id=0, has_side_effects=True),
        )(queries, keys, values, block_pairs.transpose(0, 3, 1, 2))

    rows_spec = P(("groups", "pb", "ka"), None)
    return jax.shard_map(
        local, mesh=mesh,
        in_specs=(rows_spec, rows_spec, rows_spec, P("groups", "pb", None, None)),
        out_specs=rows_spec, check_vma=False,
    )
```

```python
import functools
import math

import jax
import jax.numpy as jnp
from jax import lax
from jax.experimental import pallas as pl
from jax.experimental.pallas import tpu as pltpu
from jax.sharding import PartitionSpec as P

HEAD = 128
BLOCK = 128
STATS = 16
NEGATIVE_FILL = -1e30
EXP2_SCALE = HEAD ** (-0.5) * math.log2(math.e)
MESH = pl.DeviceIdType.MESH


def dot(a, b):
    return lax.dot_general(a, b, (((1,), (0,)), ((), ())), preferred_element_type=jnp.float32)


def kernel(
    n_pb, n_ka, width, cut, q_ref, k_ref, v_ref, pairs_ref, out_ref,
    qbuf, kbuf, vbuf, codes, marks, qturned, vturned, peak, total, accum, osend, orecv, mrecv, obuf,
    hop_send, query_send, query_recv, code_send, code_recv, side_send, kv_recv,
    swap_send, out_send, out_recv, merge_recv, local_sem,
):
    rows = q_ref.shape[0]
    tile = n_ka * rows
    blocks = rows // BLOCK
    n_y = width
    n_z = n_pb // n_y
    core = lax.axis_index("ka")
    place = lax.axis_index("pb")
    z, y = place // n_y, place % n_y
    other = 1 - core
    far_y = 1 - y
    across = z * n_y + far_y
    has_left, has_right = z > 0, z < n_z - 1
    piece = rows // cut

    barrier = pltpu.get_barrier_semaphore()

    def greet(pb, ka):
        pl.semaphore_signal(barrier, inc=1, device_id={"pb": pb, "ka": ka}, device_id_type=MESH)

    at_end = jnp.logical_not(jnp.logical_and(has_left, has_right))
    for ka in range(n_ka):
        @pl.when(has_left)
        def _():
            greet(place - n_y, ka)

        @pl.when(has_right)
        def _():
            greet(place + n_y, ka)

        greet(across, ka)
    greet(place, other)

    def columns(head):
        return pl.ds(pl.multiple_of(head * HEAD, HEAD), HEAD)

    def rows_of(ka):
        return pl.ds(pl.multiple_of(ka * rows, BLOCK), rows)

    my_rows, other_rows = rows_of(core), rows_of(other)

    stage = [
        pltpu.make_async_copy(k_ref.at[:, columns(core)], kbuf.at[y, my_rows], local_sem.at[0]),
        pltpu.make_async_copy(q_ref.at[:, columns(core)], qbuf.at[z, my_rows], local_sem.at[1]),
        pltpu.make_async_copy(v_ref.at[:, columns(core)], vbuf.at[y, my_rows], local_sem.at[2]),
    ]
    for item in stage:
        item.start()

    def remote(source, target, send_sem, recv_sem, **device):
        return pltpu.make_async_remote_copy(
            src_ref=source, dst_ref=target, send_sem=send_sem, recv_sem=recv_sem,
            device_id=device, device_id_type=MESH,
        )

    block_of_row = lax.broadcasted_iota(jnp.int32, (tile, HEAD), 0) // BLOCK
    lane = lax.broadcasted_iota(jnp.int32, (tile, HEAD), 1)
    for side in range(n_y):
        here = lane == block_of_row + side * n_ka * blocks
        marks[side] = jnp.where(here, 1.0, 0.0).astype(marks.dtype)
    pad = qturned.shape[1] - HEAD - STATS
    for layer in range(n_z):
        qturned[layer, pl.ds(HEAD + STATS, pad), :] = jnp.zeros((pad, tile), qturned.dtype)

    beside = has_left.astype(jnp.int32) + has_right.astype(jnp.int32)
    pl.semaphore_wait(barrier, n_ka * (1 + beside) + 1)

    def query_part(layer, ka, part):
        return qbuf.at[layer, pl.ds(pl.multiple_of(ka * rows + part * piece, 16), piece)]

    def hop(way, head, part):
        return remote(
            q_ref.at[pl.ds(part * piece, piece), columns(head)], query_part(z, core, part),
            hop_send.at[way, head, part], query_recv.at[z, core, part],
            pb=place + (n_y if way else -n_y), ka=head,
        )

    def hops(act):
        for part in range(cut):
            for way, there in ((0, has_left), (1, has_right)):
                @pl.when(there)
                def _():
                    for head in range(n_ka):
                        act(hop(way, head, part))

    def side_copy(which, head):
        source, target = ((k_ref, kbuf), (v_ref, vbuf))[which]
        return remote(
            source.at[:, columns(head)], target.at[y, my_rows],
            side_send.at[which, head], kv_recv.at[which, y, core], pb=across, ka=head,
        )

    def swap(which):
        source, target = (
            (k_ref, kbuf.at[y, my_rows]), (v_ref, vbuf.at[y, my_rows]), (q_ref, qbuf.at[z, my_rows]),
        )[which]
        recv = query_recv.at[z, core, 0] if which == 2 else kv_recv.at[which, y, core]
        return remote(
            source.at[:, columns(other)], target, swap_send.at[which], recv, ka=other,
        )

    def code_hop(way):
        return remote(
            pairs_ref.at[core], codes.at[z], code_send.at[z, way], code_recv.at[z],
            pb=place + (n_y if way else -n_y),
        )

    def code_hops(act):
        for way, there in ((0, has_left), (1, has_right)):
            @pl.when(there)
            def _():
                act(code_hop(way))

    hops(lambda item: item.start())
    for which in range(2):
        for head in range(n_ka):
            side_copy(which, head).start()
    for which in (0, 2, 1):
        swap(which).start()
    code_hops(lambda item: item.start())

    def wait_kv(which, side, ka):
        target = (kbuf, vbuf)[which].at[side, rows_of(ka)]
        remote(target, target, side_send.at[which, 0], kv_recv.at[which, side, ka], ka=other).wait_recv()

    row = lax.broadcasted_iota(jnp.int32, (STATS, tile), 0)
    shards = pairs_ref.shape[3]
    pick = (
        lax.broadcasted_iota(jnp.int32, (STATS, shards), 1)
        == lax.broadcasted_iota(jnp.int32, (STATS, shards), 0) // blocks + z * n_y * n_ka
    )
    pick = jnp.where(pick, 1.0, 0.0).astype(jnp.bfloat16)
    wanted = lax.broadcasted_iota(jnp.int32, (STATS, tile), 1) // BLOCK * blocks + row % blocks
    wanted = wanted.astype(jnp.float32)

    def prepare(layer, listed):
        spread = lax.dot_general(
            pick, listed.astype(jnp.float32).astype(jnp.bfloat16), (((1,), (1,)), ((), ())),
            preferred_element_type=jnp.float32,
        )
        hit = None
        for slot in range(listed.shape[0]):
            same = jnp.broadcast_to(spread[:, slot : slot + 1], (STATS, tile)) == wanted
            hit = same if hit is None else hit | same
        qturned[layer, pl.ds(HEAD, STATS), :] = jnp.where(hit, 0.0, NEGATIVE_FILL).astype(qturned.dtype)
        qturned[layer, pl.ds(0, HEAD), :] = qbuf[layer].T

    def scores_of(layer, ka, side):
        keys = jnp.concatenate([kbuf[side], marks[side]], axis=1)
        return dot(keys, qturned[layer, :, pl.ds(ka * rows, rows)])

    def first_half(layer):
        for ka in range(n_ka):
            span = pl.ds(ka * rows, rows)
            scores = scores_of(layer, ka, y)
            top = scores.max(0, keepdims=True)
            chances = jnp.exp2((scores - top) * EXP2_SCALE)
            peak[layer, :, span] = top
            total[layer, :, span] = chances.sum(0, keepdims=True)
            accum[layer, :, span] = dot(vturned[y], chances.astype(jnp.bfloat16))

    stat_row = lax.broadcasted_iota(jnp.int32, (STATS, rows), 0)

    def second_half(layer, ka):
        span = pl.ds(ka * rows, rows)
        scores = scores_of(layer, ka, far_y)
        before = peak[layer, :, span]
        top = jnp.maximum(before, scores.max(0, keepdims=True))
        rescale = jnp.exp2((before - top) * EXP2_SCALE)
        chances = jnp.exp2((scores - top) * EXP2_SCALE)
        whole = total[layer, :, span] * rescale + chances.sum(0, keepdims=True)
        mixed = accum[layer, :, span] * rescale + dot(vturned[far_y], chances.astype(jnp.bfloat16))
        osend[layer, ka, pl.ds(0, HEAD), :] = (mixed * (1.0 / whole)).astype(osend.dtype)
        put_level(osend.at[layer, ka], top * EXP2_SCALE + jnp.log2(whole))

    def put_level(ref, level):
        high = level.astype(jnp.bfloat16).astype(jnp.float32)
        middle = (level - high).astype(jnp.bfloat16).astype(jnp.float32)
        low = level - high - middle
        stats = jnp.where(stat_row == 0, high, jnp.where(stat_row == 1, middle, jnp.where(stat_row == 2, low, 0.0)))
        ref[pl.ds(HEAD, STATS), :] = stats.astype(ref.dtype)

    def level_of(ref):
        stats = ref[pl.ds(HEAD, STATS), :].astype(jnp.float32)
        return stats[0:1] + stats[1:2] + stats[2:3]

    def merge(into, ref):
        mine, theirs = level_of(into), level_of(ref)
        top = jnp.maximum(mine, theirs)
        share, their_share = jnp.exp2(mine - top), jnp.exp2(theirs - top)
        whole = share + their_share
        scale = 1.0 / whole
        mixed = into[pl.ds(0, HEAD), :].astype(jnp.float32) * (share * scale)
        mixed = mixed + ref[pl.ds(0, HEAD), :].astype(jnp.float32) * (their_share * scale)
        into[pl.ds(0, HEAD), :] = mixed.astype(into.dtype)
        put_level(into, top + jnp.log2(whole))

    def straight(layer, ka):
        return remote(
            osend.at[layer, ka], orecv.at[z, core], out_send.at[layer, ka], out_recv.at[z, core],
            pb=layer * n_y + y, ka=ka,
        )

    def between(layer, ka):
        side = jnp.where(layer < z, 0, 1)
        return remote(
            osend.at[layer, ka], mrecv.at[side, ka], out_send.at[layer, ka], merge_recv.at[side, ka],
            pb=jnp.where(layer < z, place - n_y, place + n_y),
        )

    def two_away(layer):
        return jnp.logical_or(layer == z + 2, layer == z - 2)

    def give(layer, ka):
        @pl.when(two_away(layer))
        def _():
            between(layer, ka).start()

        @pl.when(jnp.logical_not(two_away(layer)))
        def _():
            straight(layer, ka).start()

    def give_other():
        return remote(
            osend.at[z, other], orecv.at[z, core], out_send.at[z, other], out_recv.at[z, core], ka=other,
        )

    shorter = jnp.minimum(z, n_z - 1 - z)
    long_right = z < n_z - 1 - z

    def layer_at(turn):
        both = turn <= 2 * shorter
        away = jnp.where(both, (turn + 1) // 2, turn - shorter)
        longer = jnp.where(both, turn % 2, 1)
        step = away * (2 * longer - 1)
        return jnp.where(long_right, z + step, z - step)

    def onward(layer):
        return jnp.logical_or(
            jnp.logical_and(layer < z, has_right), jnp.logical_and(layer > z, has_left)
        )

    def forward(layer, ka, part):
        ref = query_part(layer, ka, part)
        return remote(
            ref, ref, query_send.at[layer, ka, part], query_recv.at[layer, ka, part],
            pb=jnp.where(layer < z, place + n_y, place - n_y),
        )

    def code_forward(layer):
        return remote(
            codes.at[layer], codes.at[layer], code_send.at[layer, 0], code_recv.at[layer],
            pb=jnp.where(layer < z, place + n_y, place - n_y),
        )

    def take(layer, parts=tuple(range(cut))):
        for part in parts:
            for ka in (core, other):
                forward(layer, ka, part).wait_recv()

                @pl.when(onward(layer))
                def _():
                    forward(layer, ka, part).start()

            if part == 0:
                code_forward(layer).wait_recv()

                @pl.when(onward(layer))
                def _():
                    code_forward(layer).start()

    def ready(layer):
        prepare(layer, codes[layer, :, 0, :])

    for item in stage:
        item.wait()
    wait_kv(0, y, other)
    incoming = qbuf.at[z, other_rows]
    remote(incoming, incoming, swap_send.at[2], query_recv.at[z, other, 0], ka=other).wait_recv()
    prepare(z, pairs_ref[core, :, 0, :])
    wait_kv(1, y, other)
    vturned[y] = vbuf[y].T
    first_half(z)

    middle = jnp.logical_not(at_end)
    one, two, three = layer_at(1), layer_at(2), layer_at(3)
    take(one)

    @pl.when(middle)
    def _():
        take(two)

    ready(one)
    first_half(one)

    @pl.when(middle)
    def _():
        take(three, (0,))

    @pl.when(at_end)
    def _():
        take(two)

    ready(two)
    first_half(two)

    @pl.when(middle)
    def _():
        take(three, tuple(range(1, cut)))
        ready(three)
        first_half(three)

    for which in range(2):
        for ka in range(n_ka):
            wait_kv(which, far_y, ka)
    vturned[far_y] = vbuf[far_y].T
    early = jnp.where(at_end, two, three)
    for ka in range(n_ka):
        second_half(early, ka)
        give(early, ka)
    for ka in range(n_ka):
        second_half(one, ka)

        @pl.when(at_end)
        def _():
            give(one, ka)

    @pl.when(at_end)
    def _():
        take(three)
        ready(three)
        first_half(three)

    late = jnp.where(at_end, three, two)
    for ka in range(n_ka):
        second_half(late, ka)

        @pl.when(at_end)
        def _():
            give(late, ka)

    if n_z > 4:
        def visit(turn, carry):
            layer = layer_at(turn)
            take(layer)
            ready(layer)
            first_half(layer)
            for ka in range(n_ka):
                second_half(layer, ka)
                give(layer, ka)
            return carry

        lax.fori_loop(4, n_z, visit, 0)

    for ka in range(n_ka):
        second_half(z, ka)
    give_other().start()

    @pl.when(middle)
    def _():
        for layer in (one, two):
            side = jnp.where(layer < z, 0, 1)
            for ka in range(n_ka):
                ref = mrecv.at[side, ka]
                remote(ref, ref, out_send.at[layer, ka], merge_recv.at[side, ka], ka=other).wait_recv()
                merge(osend.at[layer, ka], ref)
                straight(layer, ka).start()

    def wait_out(layer, head):
        ref = orecv.at[layer, head]
        remote(ref, ref, out_send.at[z, 0], out_recv.at[layer, head], ka=other).wait_recv()

    wait_out(z, other)
    if n_z > 4:
        def gather(turn, carry):
            layer = layer_at(turn)

            @pl.when(jnp.logical_not(two_away(layer)))
            def _():
                for head in (core, other):
                    wait_out(layer, head)
                merge(osend.at[z, core], orecv.at[layer, core])
                merge(orecv.at[z, other], orecv.at[layer, other])

            return carry

        lax.fori_loop(4, n_z, gather, 0)
    sources = (one, late)
    for layer in sources:
        for head in range(n_ka):
            wait_out(layer, head)

    keeps = []
    for index, head in enumerate((core, other)):
        refs = [orecv.at[z, head] if index else osend.at[z, core]]
        refs += [orecv.at[layer, head] for layer in sources]
        parts = [(ref, level_of(ref)) for ref in refs]
        top = functools.reduce(jnp.maximum, [level for _, level in parts])
        shares = [jnp.exp2(level - top) for _, level in parts]
        scale = 1.0 / functools.reduce(jnp.add, shares)
        mixed = None
        for (ref, _), share in zip(parts, shares):
            term = ref[pl.ds(0, HEAD), :].astype(jnp.float32) * (share * scale)
            mixed = term if mixed is None else mixed + term
        obuf[index] = mixed.T.astype(obuf.dtype)
        keep = pltpu.make_async_copy(obuf.at[index], out_ref.at[:, columns(head)], local_sem.at[3 + index])
        keep.start()
        keeps.append(keep)

    hops(lambda item: item.wait_send())
    for which in range(2):
        for head in range(n_ka):
            side_copy(which, head).wait_send()
    for which in range(3):
        swap(which).wait_send()
    code_hops(lambda item: item.wait_send())

    def drain(turn, carry):
        layer = layer_at(turn)
        for ka in range(n_ka):
            straight(layer, ka).wait_send()

        @pl.when(onward(layer))
        def _():
            code_forward(layer).wait_send()
            for ka in range(n_ka):
                for part in range(cut):
                    forward(layer, ka, part).wait_send()

        return carry

    lax.fori_loop(1, n_z, drain, 0)
    give_other().wait_send()
    for keep in keeps:
        keep.wait()


def solution(mesh):
    n_pb, n_ka = mesh.shape["pb"], mesh.shape["ka"]
    width = 2
    cut = 2

    def local(queries, keys, values, block_pairs):
        rows = queries.shape[0]
        tile = n_ka * rows
        shards, most = block_pairs.shape[2:]
        n_z = n_pb // width
        anywhere = pl.BlockSpec(memory_space=pl.ANY)
        half = jnp.bfloat16
        dma = pltpu.SemaphoreType.DMA
        return pl.pallas_call(
            functools.partial(kernel, n_pb, n_ka, width, cut),
            out_shape=jax.ShapeDtypeStruct(queries.shape, queries.dtype),
            in_specs=[anywhere, anywhere, anywhere, pl.BlockSpec(memory_space=pltpu.VMEM)],
            out_specs=anywhere,
            scratch_shapes=[
                pltpu.VMEM((n_z, tile, HEAD), half),
                pltpu.VMEM((width, tile, HEAD), half),
                pltpu.VMEM((width, tile, HEAD), half),
                pltpu.VMEM((n_z, most, 1, shards), jnp.int32),
                pltpu.VMEM((width, tile, HEAD), half),
                pltpu.VMEM((n_z, 2 * HEAD, tile), half),
                pltpu.VMEM((width, HEAD, tile), half),
                pltpu.VMEM((n_z, 1, tile), jnp.float32),
                pltpu.VMEM((n_z, 1, tile), jnp.float32),
                pltpu.VMEM((n_z, HEAD, tile), jnp.float32),
                pltpu.VMEM((n_z, n_ka, HEAD + STATS, rows), half),
                pltpu.VMEM((n_z, n_ka, HEAD + STATS, rows), half),
                pltpu.VMEM((2, n_ka, HEAD + STATS, rows), half),
                pltpu.VMEM((n_ka, rows, HEAD), half),
                dma((2, n_ka, cut)),
                dma((n_z, n_ka, cut)),
                dma((n_z, n_ka, cut)),
                dma((n_z, 2)),
                dma((n_z,)),
                dma((2, n_ka)),
                dma((2, width, n_ka)),
                dma((3,)),
                dma((n_z, n_ka)),
                dma((n_z, n_ka)),
                dma((2, n_ka)),
                dma((5,)),
            ],
            compiler_params=pltpu.CompilerParams(
                collective_id=0, has_side_effects=True, vmem_limit_bytes=56 * 1024 * 1024
            ),
        )(queries, keys, values, block_pairs.transpose(0, 3, 1, 2))

    rows_spec = P(("groups", "pb", "ka"), None)
    return jax.shard_map(
        local, mesh=mesh,
        in_specs=(rows_spec, rows_spec, rows_spec, P("groups", "pb", None, None)),
        out_specs=rows_spec, check_vma=False,
    )
```

```python
import functools
import math

import jax
import jax.numpy as jnp
from jax import lax
from jax.experimental import pallas as pl
from jax.experimental.pallas import tpu as pltpu
from jax.sharding import PartitionSpec as P

HEAD = 128
BLOCK = 128
STATS = 16
NEGATIVE_FILL = -1e30
EXP2_SCALE = HEAD ** (-0.5) * math.log2(math.e)
MESH = pl.DeviceIdType.MESH


def dot(a, b):
    return lax.dot_general(a, b, (((1,), (0,)), ((), ())), preferred_element_type=jnp.float32)


def kernel(
    n_pb, n_ka, width, cut, q_ref, k_ref, v_ref, pairs_ref, out_ref,
    qbuf, kbuf, vbuf, kend, vend, codes, marks, qturned, vturned, peak, total, accum, osend, orecv, mrecv, obuf,
    hop_send, query_send, query_recv, code_send, code_recv, side_send, kv_recv,
    swap_send, out_send, out_recv, merge_recv, end_send, end_recv, local_sem,
):
    rows = q_ref.shape[0]
    tile = n_ka * rows
    blocks = rows // BLOCK
    n_y = width
    n_z = n_pb // n_y
    core = lax.axis_index("ka")
    place = lax.axis_index("pb")
    z, y = place // n_y, place % n_y
    other = 1 - core
    far_y = 1 - y
    across = z * n_y + far_y
    has_left, has_right = z > 0, z < n_z - 1
    piece = rows // cut

    barrier = pltpu.get_barrier_semaphore()

    def greet(pb, ka):
        pl.semaphore_signal(barrier, inc=1, device_id={"pb": pb, "ka": ka}, device_id_type=MESH)

    at_end = jnp.logical_not(jnp.logical_and(has_left, has_right))
    by_end = jnp.logical_or(z == 1, z == n_z - 2)
    last = jnp.where(z < n_z - 1 - z, 0, n_z - 1)
    inner = jnp.where(has_left, place - n_y, place + n_y)
    hops_left, hops_right = z > 1, z < n_z - 2
    hops_left = jnp.logical_or(hops_left, z == n_z - 1)
    hops_right = jnp.logical_or(hops_right, z == 0)
    for ka in range(n_ka):
        @pl.when(has_left)
        def _():
            greet(place - n_y, ka)

        @pl.when(has_right)
        def _():
            greet(place + n_y, ka)

        greet(across, ka)
    greet(place, other)

    def columns(head):
        return pl.ds(pl.multiple_of(head * HEAD, HEAD), HEAD)

    def rows_of(ka):
        return pl.ds(pl.multiple_of(ka * rows, BLOCK), rows)

    my_rows, other_rows = rows_of(core), rows_of(other)

    stage = [
        pltpu.make_async_copy(k_ref.at[:, columns(core)], kbuf.at[y, my_rows], local_sem.at[0]),
        pltpu.make_async_copy(q_ref.at[:, columns(core)], qbuf.at[z, my_rows], local_sem.at[1]),
        pltpu.make_async_copy(v_ref.at[:, columns(core)], vbuf.at[y, my_rows], local_sem.at[2]),
    ]
    for item in stage:
        item.start()

    def remote(source, target, send_sem, recv_sem, **device):
        return pltpu.make_async_remote_copy(
            src_ref=source, dst_ref=target, send_sem=send_sem, recv_sem=recv_sem,
            device_id=device, device_id_type=MESH,
        )

    block_of_row = lax.broadcasted_iota(jnp.int32, (tile, HEAD), 0) // BLOCK
    lane = lax.broadcasted_iota(jnp.int32, (tile, HEAD), 1)
    for side in range(n_y):
        here = lane == block_of_row + side * n_ka * blocks
        marks[0, side] = jnp.where(here, 1.0, 0.0).astype(marks.dtype)
        there = lane == block_of_row + side * n_ka * blocks + STATS
        marks[1, side] = jnp.where(there, 1.0, 0.0).astype(marks.dtype)
    pad = qturned.shape[1] - HEAD - STATS
    for layer in range(n_z):
        qturned[layer, pl.ds(HEAD + STATS, pad), :] = jnp.zeros((pad, tile), qturned.dtype)

    beside = has_left.astype(jnp.int32) + has_right.astype(jnp.int32)
    pl.semaphore_wait(barrier, n_ka * (1 + beside) + 1)

    def query_part(layer, ka, part):
        return qbuf.at[layer, pl.ds(pl.multiple_of(ka * rows + part * piece, 16), piece)]

    def hop(way, head, part):
        return remote(
            q_ref.at[pl.ds(part * piece, piece), columns(head)], query_part(z, core, part),
            hop_send.at[way, head, part], query_recv.at[z, core, part],
            pb=place + (n_y if way else -n_y), ka=head,
        )

    def hops(act):
        for part in range(cut):
            for way, there in ((0, hops_left), (1, hops_right)):
                @pl.when(there)
                def _():
                    for head in (core, other):
                        act(hop(way, head, part))

    def side_copy(which, head):
        source, target = ((k_ref, kbuf), (v_ref, vbuf))[which]
        return remote(
            source.at[:, columns(head)], target.at[y, my_rows],
            side_send.at[which, head], kv_recv.at[which, y, core], pb=across, ka=head,
        )

    def end_copy(which, head):
        source, target = ((k_ref, kend), (v_ref, vend))[which]
        return remote(
            source.at[:, columns(head)], target.at[y, my_rows],
            end_send.at[which, head], end_recv.at[which, y, core], pb=inner, ka=head,
        )

    def end_pass(which, ka):
        ref = (kend, vend)[which].at[y, rows_of(ka)]
        return remote(ref, ref, end_send.at[which, ka], end_recv.at[which, y, ka], pb=across)

    def wait_end(which, side, ka):
        ref = (kend, vend)[which].at[side, rows_of(ka)]
        remote(ref, ref, end_send.at[which, ka], end_recv.at[which, side, ka], pb=across).wait_recv()

    def pass_end(which):
        @pl.when(by_end)
        def _():
            for ka in (core, other):
                wait_end(which, y, ka)
                end_pass(which, ka).start()

    def swap(which):
        source, target = (
            (k_ref, kbuf.at[y, my_rows]), (v_ref, vbuf.at[y, my_rows]), (q_ref, qbuf.at[z, my_rows]),
        )[which]
        recv = query_recv.at[z, core, 0] if which == 2 else kv_recv.at[which, y, core]
        return remote(
            source.at[:, columns(other)], target, swap_send.at[which], recv, ka=other,
        )

    def code_hop(way):
        return remote(
            pairs_ref.at[core], codes.at[z], code_send.at[z, way], code_recv.at[z],
            pb=place + (n_y if way else -n_y),
        )

    def code_hops(act):
        for way, there in ((0, hops_left), (1, hops_right)):
            @pl.when(there)
            def _():
                act(code_hop(way))

    hops(lambda item: item.start())
    for which in range(2):
        for head in (core, other):
            side_copy(which, head).start()
    for which in (0, 2, 1):
        swap(which).start()
    code_hops(lambda item: item.start())

    @pl.when(at_end)
    def _():
        for which in range(2):
            for head in (core, other):
                end_copy(which, head).start()


    def wait_kv(which, side, ka):
        target = (kbuf, vbuf)[which].at[side, rows_of(ka)]
        remote(target, target, side_send.at[which, 0], kv_recv.at[which, side, ka], ka=other).wait_recv()

    row = lax.broadcasted_iota(jnp.int32, (STATS, tile), 0)
    shards = pairs_ref.shape[3]
    def pick_of(owner):
        pick = (
            lax.broadcasted_iota(jnp.int32, (STATS, shards), 1)
            == lax.broadcasted_iota(jnp.int32, (STATS, shards), 0) // blocks + owner * n_y * n_ka
        )
        return jnp.where(pick, 1.0, 0.0).astype(jnp.bfloat16)

    mine = pick_of(z)
    wanted = lax.broadcasted_iota(jnp.int32, (STATS, tile), 1) // BLOCK * blocks + row % blocks
    wanted = wanted.astype(jnp.float32)

    def mask(layer, listed, pick, start):
        spread = lax.dot_general(
            pick, listed.astype(jnp.float32).astype(jnp.bfloat16), (((1,), (1,)), ((), ())),
            preferred_element_type=jnp.float32,
        )
        hit = None
        for slot in range(listed.shape[0]):
            same = jnp.broadcast_to(spread[:, slot : slot + 1], (STATS, tile)) == wanted
            hit = same if hit is None else hit | same
        qturned[layer, pl.ds(start, STATS), :] = jnp.where(hit, 0.0, NEGATIVE_FILL).astype(qturned.dtype)

    def prepare(layer, listed):
        mask(layer, listed, mine, HEAD)
        qturned[layer, pl.ds(0, HEAD), :] = qbuf[layer].T

    def scores_of(layer, side):
        keys = jnp.concatenate([kbuf[side], marks[0, side]], axis=1)
        return dot(keys, qturned[layer])

    def first_half(layer):
        scores = scores_of(layer, y)
        top = scores.max(0, keepdims=True)
        chances = jnp.exp2((scores - top) * EXP2_SCALE)
        peak[layer] = top
        total[layer] = chances.sum(0, keepdims=True)
        accum[layer] = dot(vturned[y], chances.astype(jnp.bfloat16))

    stat_row = lax.broadcasted_iota(jnp.int32, (STATS, rows), 0)

    def put(layer, top, whole, mixed):
        mixed = mixed * (1.0 / whole)
        level = top * EXP2_SCALE + jnp.log2(whole)
        for ka in range(n_ka):
            osend[layer, ka, pl.ds(0, HEAD), :] = mixed[:, ka * rows : (ka + 1) * rows].astype(osend.dtype)
            put_level(osend.at[layer, ka], level[:, ka * rows : (ka + 1) * rows])

    def second_state(layer):
        scores = scores_of(layer, far_y)
        before = peak[layer]
        top = jnp.maximum(before, scores.max(0, keepdims=True))
        rescale = jnp.exp2((before - top) * EXP2_SCALE)
        chances = jnp.exp2((scores - top) * EXP2_SCALE)
        whole = total[layer] * rescale + chances.sum(0, keepdims=True)
        return top, whole, accum[layer] * rescale + dot(vturned[far_y], chances.astype(jnp.bfloat16))

    def second_half(layer):
        put(layer, *second_state(layer))

    def whole_tile(layer, keys, hints, columns_of):
        keys = jnp.concatenate([keys[...], hints[...]], axis=2).reshape(n_y * tile, 2 * HEAD)
        scores = dot(keys, qturned[layer])
        top = scores.max(0, keepdims=True)
        chances = jnp.exp2((scores - top) * EXP2_SCALE)
        whole = chances.sum(0, keepdims=True)
        chances = chances.astype(jnp.bfloat16)
        mixed = dot(columns_of(0), chances[:tile])
        for side in range(1, n_y):
            mixed = mixed + dot(columns_of(side), chances[side * tile : (side + 1) * tile])
        return top, whole, mixed

    def both_halves(layer):
        put(layer, *whole_tile(layer, kbuf, marks.at[0], lambda side: vturned[side]))

    def end_tile():
        top, whole, mixed = whole_tile(z, kend, marks.at[1], lambda side: vend[side].T)
        before = peak[z]
        after = jnp.maximum(before, top)
        old, new = jnp.exp2((before - after) * EXP2_SCALE), jnp.exp2((top - after) * EXP2_SCALE)
        put(z, after, total[z] * old + whole * new, accum[z] * old + mixed * new)

    def put_level(ref, level):
        high = level.astype(jnp.bfloat16).astype(jnp.float32)
        middle = (level - high).astype(jnp.bfloat16).astype(jnp.float32)
        low = level - high - middle
        stats = jnp.where(stat_row == 0, high, jnp.where(stat_row == 1, middle, jnp.where(stat_row == 2, low, 0.0)))
        ref[pl.ds(HEAD, STATS), :] = stats.astype(ref.dtype)

    def level_of(ref):
        stats = ref[pl.ds(HEAD, STATS), :].astype(jnp.float32)
        return stats[0:1] + stats[1:2] + stats[2:3]

    def merge(into, ref):
        mine, theirs = level_of(into), level_of(ref)
        top = jnp.maximum(mine, theirs)
        share, their_share = jnp.exp2(mine - top), jnp.exp2(theirs - top)
        whole = share + their_share
        scale = 1.0 / whole
        mixed = into[pl.ds(0, HEAD), :].astype(jnp.float32) * (share * scale)
        mixed = mixed + ref[pl.ds(0, HEAD), :].astype(jnp.float32) * (their_share * scale)
        into[pl.ds(0, HEAD), :] = mixed.astype(into.dtype)
        put_level(into, top + jnp.log2(whole))

    def straight(layer, ka):
        return remote(
            osend.at[layer, ka], orecv.at[z, core], out_send.at[layer, ka], out_recv.at[z, core],
            pb=layer * n_y + y, ka=ka,
        )

    def between(layer, ka):
        side = jnp.where(layer < z, 0, 1)
        return remote(
            osend.at[layer, ka], mrecv.at[side, ka], out_send.at[layer, ka], merge_recv.at[side, ka],
            pb=jnp.where(layer < z, place - n_y, place + n_y),
        )

    def two_away(layer):
        return jnp.logical_or(layer == z + 2, layer == z - 2)

    def give(layer, ka):
        @pl.when(two_away(layer))
        def _():
            between(layer, ka).start()

        @pl.when(jnp.logical_not(two_away(layer)))
        def _():
            straight(layer, ka).start()

    def give_other():
        return remote(
            osend.at[z, other], orecv.at[z, core], out_send.at[z, other], out_recv.at[z, core], ka=other,
        )

    shorter = jnp.minimum(z, n_z - 1 - z)
    long_right = z < n_z - 1 - z

    def layer_at(turn):
        both = turn <= 2 * shorter
        away = jnp.where(both, (turn + 1) // 2, turn - shorter)
        longer = jnp.where(both, turn % 2, 1)
        step = away * (2 * longer - 1)
        return jnp.where(long_right, z + step, z - step)

    def onward(layer):
        return jnp.logical_or(
            jnp.logical_and(layer < z, has_right), jnp.logical_and(layer > z, has_left)
        )

    def forward(layer, ka, part):
        ref = query_part(layer, ka, part)
        return remote(
            ref, ref, query_send.at[layer, ka, part], query_recv.at[layer, ka, part],
            pb=jnp.where(layer < z, place + n_y, place - n_y),
        )

    def code_forward(layer):
        return remote(
            codes.at[layer], codes.at[layer], code_send.at[layer, 0], code_recv.at[layer],
            pb=jnp.where(layer < z, place + n_y, place - n_y),
        )

    def take(layer, parts=tuple(range(cut))):
        for part in parts:
            for ka in (core, other):
                forward(layer, ka, part).wait_recv()

                @pl.when(onward(layer))
                def _():
                    forward(layer, ka, part).start()

            if part == 0:
                code_forward(layer).wait_recv()

                @pl.when(onward(layer))
                def _():
                    code_forward(layer).start()

    def ready(layer):
        prepare(layer, codes[layer, :, 0, :])

    for item in stage:
        item.wait()
    wait_kv(0, y, other)
    incoming = qbuf.at[z, other_rows]
    remote(incoming, incoming, swap_send.at[2], query_recv.at[z, other, 0], ka=other).wait_recv()
    prepare(z, pairs_ref[core, :, 0, :])
    wait_kv(1, y, other)
    vturned[y] = vbuf[y].T
    first_half(z)

    middle = jnp.logical_not(at_end)
    one, two, three = layer_at(1), layer_at(2), layer_at(3)

    @pl.when(middle)
    def _():
        take(one)
        take(two)
        ready(one)
        first_half(one)
        take(three, (0,))
        ready(two)
        first_half(two)
        take(three, tuple(range(1, cut)))
        ready(three)

    @pl.when(at_end)
    def _():
        take(two)
        ready(two)
        first_half(two)

    pass_end(0)
    for which in range(2):
        for ka in range(n_ka):
            wait_kv(which, far_y, ka)
    vturned[far_y] = vbuf[far_y].T

    def give_all(layer):
        for ka in (core, other):
            give(layer, ka)

    @pl.when(middle)
    def _():
        both_halves(three)
        give_all(three)
        second_half(one)
        pass_end(1)
        second_half(two)

    @pl.when(at_end)
    def _():
        second_half(two)
        give_all(two)
        take(three)
        ready(three)
        both_halves(three)
        give_all(three)

    late = jnp.where(at_end, three, two)
    final = jnp.where(by_end, one, late)

    if n_z > 4:
        def visit(turn, carry):
            layer = layer_at(turn)
            take(layer)
            ready(layer)
            both_halves(layer)
            give_all(layer)
            return carry

        lax.fori_loop(4, n_z, visit, 0)

    @pl.when(jnp.logical_not(by_end))
    def _():
        second_half(z)
        give_other().start()

    @pl.when(by_end)
    def _():
        peak[z], total[z], accum[z] = second_state(z)

    @pl.when(middle)
    def _():
        for layer in (one, two):
            side = jnp.where(layer < z, 0, 1)
            for ka in range(n_ka):
                ref = mrecv.at[side, ka]
                remote(ref, ref, out_send.at[layer, ka], merge_recv.at[side, ka], ka=other).wait_recv()
                merge(osend.at[layer, ka], ref)
                straight(layer, ka).start()

    @pl.when(by_end)
    def _():
        mask(z, pairs_ref[core, :, 0, :], pick_of(last), HEAD + STATS)
        for which in range(2):
            for ka in range(n_ka):
                wait_end(which, far_y, ka)
        end_tile()
        give_other().start()

    def wait_out(layer, head):
        ref = orecv.at[layer, head]
        remote(ref, ref, out_send.at[z, 0], out_recv.at[layer, head], ka=other).wait_recv()

    wait_out(z, other)
    if n_z > 4:
        def gather(turn, carry):
            layer = layer_at(turn)

            @pl.when(jnp.logical_not(two_away(layer)))
            def _():
                for head in (core, other):
                    wait_out(layer, head)
                merge(osend.at[z, core], orecv.at[layer, core])
                merge(orecv.at[z, other], orecv.at[layer, other])

            return carry

        lax.fori_loop(4, n_z, gather, 0)
    @pl.when(jnp.logical_not(by_end))
    def _():
        for head in (core, other):
            wait_out(one, head)
        merge(osend.at[z, core], orecv.at[one, core])
        merge(orecv.at[z, other], orecv.at[one, other])

    keeps = []
    for index, head in enumerate((core, other)):
        wait_out(final, head)
        refs = [orecv.at[z, head] if index else osend.at[z, core], orecv.at[final, head]]
        parts = [(ref, level_of(ref)) for ref in refs]
        top = functools.reduce(jnp.maximum, [level for _, level in parts])
        shares = [jnp.exp2(level - top) for _, level in parts]
        scale = 1.0 / functools.reduce(jnp.add, shares)
        mixed = None
        for (ref, _), share in zip(parts, shares):
            term = ref[pl.ds(0, HEAD), :].astype(jnp.float32) * (share * scale)
            mixed = term if mixed is None else mixed + term
        obuf[index] = mixed.T.astype(obuf.dtype)
        keep = pltpu.make_async_copy(obuf.at[index], out_ref.at[:, columns(head)], local_sem.at[3 + index])
        keep.start()
        keeps.append(keep)

    hops(lambda item: item.wait_send())
    for which in range(2):
        for head in range(n_ka):
            side_copy(which, head).wait_send()
    for which in range(3):
        swap(which).wait_send()
    code_hops(lambda item: item.wait_send())

    def drain(turn, carry):
        layer = layer_at(turn)

        @pl.when(jnp.logical_or(middle, turn != 1))
        def _():
            for ka in range(n_ka):
                straight(layer, ka).wait_send()

        @pl.when(onward(layer))
        def _():
            code_forward(layer).wait_send()
            for ka in range(n_ka):
                for part in range(cut):
                    forward(layer, ka, part).wait_send()

        return carry

    lax.fori_loop(1, n_z, drain, 0)

    @pl.when(at_end)
    def _():
        for which in range(2):
            for head in range(n_ka):
                end_copy(which, head).wait_send()

    @pl.when(by_end)
    def _():
        for which in range(2):
            for ka in range(n_ka):
                end_pass(which, ka).wait_send()

    give_other().wait_send()
    for keep in keeps:
        keep.wait()


def solution(mesh):
    n_pb, n_ka = mesh.shape["pb"], mesh.shape["ka"]
    width = 2
    cut = 2

    def local(queries, keys, values, block_pairs):
        rows = queries.shape[0]
        tile = n_ka * rows
        shards, most = block_pairs.shape[2:]
        n_z = n_pb // width
        anywhere = pl.BlockSpec(memory_space=pl.ANY)
        half = jnp.bfloat16
        dma = pltpu.SemaphoreType.DMA
        return pl.pallas_call(
            functools.partial(kernel, n_pb, n_ka, width, cut),
            out_shape=jax.ShapeDtypeStruct(queries.shape, queries.dtype),
            in_specs=[anywhere, anywhere, anywhere, pl.BlockSpec(memory_space=pltpu.VMEM)],
            out_specs=anywhere,
            scratch_shapes=[
                pltpu.VMEM((n_z, tile, HEAD), half),
                pltpu.VMEM((width, tile, HEAD), half),
                pltpu.VMEM((width, tile, HEAD), half),
                pltpu.VMEM((width, tile, HEAD), half),
                pltpu.VMEM((width, tile, HEAD), half),
                pltpu.VMEM((n_z, most, 1, shards), jnp.int32),
                pltpu.VMEM((2, width, tile, HEAD), half),
                pltpu.VMEM((n_z, 2 * HEAD, tile), half),
                pltpu.VMEM((width, HEAD, tile), half),
                pltpu.VMEM((n_z, 1, tile), jnp.float32),
                pltpu.VMEM((n_z, 1, tile), jnp.float32),
                pltpu.VMEM((n_z, HEAD, tile), jnp.float32),
                pltpu.VMEM((n_z, n_ka, HEAD + STATS, rows), half),
                pltpu.VMEM((n_z, n_ka, HEAD + STATS, rows), half),
                pltpu.VMEM((2, n_ka, HEAD + STATS, rows), half),
                pltpu.VMEM((n_ka, rows, HEAD), half),
                dma((2, n_ka, cut)),
                dma((n_z, n_ka, cut)),
                dma((n_z, n_ka, cut)),
                dma((n_z, 2)),
                dma((n_z,)),
                dma((2, n_ka)),
                dma((2, width, n_ka)),
                dma((3,)),
                dma((n_z, n_ka)),
                dma((n_z, n_ka)),
                dma((2, n_ka)),
                dma((2, n_ka)),
                dma((2, width, n_ka)),
                dma((5,)),
            ],
            compiler_params=pltpu.CompilerParams(
                collective_id=0, has_side_effects=True, vmem_limit_bytes=56 * 1024 * 1024
            ),
        )(queries, keys, values, block_pairs.transpose(0, 3, 1, 2))

    rows_spec = P(("groups", "pb", "ka"), None)
    return jax.shard_map(
        local, mesh=mesh,
        in_specs=(rows_spec, rows_spec, rows_spec, P("groups", "pb", None, None)),
        out_specs=rows_spec, check_vma=False,
    )
```

```python
import functools
import math

import jax
import jax.numpy as jnp
from jax import lax
from jax.experimental import pallas as pl
from jax.experimental.pallas import tpu as pltpu
from jax.sharding import PartitionSpec as P

HEAD = 128
BLOCK = 128
STATS = 16
NEGATIVE_FILL = -1e30
EXP2_SCALE = HEAD ** (-0.5) * math.log2(math.e)
MESH = pl.DeviceIdType.MESH


def dot(a, b):
    return lax.dot_general(a, b, (((1,), (0,)), ((), ())), preferred_element_type=jnp.float32)


def kernel(
    n_pb, n_ka, width, cut, q_ref, k_ref, v_ref, pairs_ref, out_ref,
    qbuf, kbuf, vbuf, kend, vend, codes, marks, qturned, vturned, peak, total, accum, osend, orecv, mrecv, obuf,
    hop_send, query_send, query_recv, code_send, code_recv, side_send, kv_recv,
    swap_send, out_send, out_recv, merge_recv, end_send, end_recv, local_sem,
):
    rows = q_ref.shape[0]
    tile = n_ka * rows
    blocks = rows // BLOCK
    n_y = width
    n_z = n_pb // n_y
    core = lax.axis_index("ka")
    place = lax.axis_index("pb")
    z, y = place // n_y, place % n_y
    other = 1 - core
    far_y = 1 - y
    across = z * n_y + far_y
    has_left, has_right = z > 0, z < n_z - 1
    piece = rows // cut

    barrier = pltpu.get_barrier_semaphore()

    def greet(pb, ka):
        pl.semaphore_signal(barrier, inc=1, device_id={"pb": pb, "ka": ka}, device_id_type=MESH)

    at_end = jnp.logical_not(jnp.logical_and(has_left, has_right))
    by_end = jnp.logical_or(z == 1, z == n_z - 2)
    last = jnp.where(z < n_z - 1 - z, 0, n_z - 1)
    inner = jnp.where(has_left, place - n_y, place + n_y)
    hops_left, hops_right = z > 1, z < n_z - 2
    hops_left = jnp.logical_or(hops_left, z == n_z - 1)
    hops_right = jnp.logical_or(hops_right, z == 0)
    for ka in range(n_ka):
        @pl.when(has_left)
        def _():
            greet(place - n_y, ka)

        @pl.when(has_right)
        def _():
            greet(place + n_y, ka)

        greet(across, ka)
    greet(place, other)

    def columns(head):
        return pl.ds(pl.multiple_of(head * HEAD, HEAD), HEAD)

    def rows_of(ka):
        return pl.ds(pl.multiple_of(ka * rows, BLOCK), rows)

    my_rows, other_rows = rows_of(core), rows_of(other)

    stage = [
        pltpu.make_async_copy(k_ref.at[:, columns(core)], kbuf.at[y, my_rows], local_sem.at[0]),
        pltpu.make_async_copy(q_ref.at[:, columns(core)], qbuf.at[z, my_rows], local_sem.at[1]),
        pltpu.make_async_copy(v_ref.at[:, columns(core)], vbuf.at[y, my_rows], local_sem.at[2]),
    ]
    for item in stage:
        item.start()

    def remote(source, target, send_sem, recv_sem, **device):
        return pltpu.make_async_remote_copy(
            src_ref=source, dst_ref=target, send_sem=send_sem, recv_sem=recv_sem,
            device_id=device, device_id_type=MESH,
        )

    block_of_row = lax.broadcasted_iota(jnp.int32, (tile, HEAD), 0) // BLOCK
    lane = lax.broadcasted_iota(jnp.int32, (tile, HEAD), 1)
    for side in range(n_y):
        here = lane == block_of_row + side * n_ka * blocks
        marks[0, side] = jnp.where(here, 1.0, 0.0).astype(marks.dtype)
        there = lane == block_of_row + side * n_ka * blocks + STATS
        marks[1, side] = jnp.where(there, 1.0, 0.0).astype(marks.dtype)
    pad = qturned.shape[1] - HEAD - STATS
    for layer in range(n_z):
        qturned[layer, pl.ds(HEAD + STATS, pad), :] = jnp.zeros((pad, tile), qturned.dtype)

    beside = has_left.astype(jnp.int32) + has_right.astype(jnp.int32)
    pl.semaphore_wait(barrier, n_ka * (1 + beside) + 1)

    def query_part(layer, ka, part):
        return qbuf.at[layer, pl.ds(pl.multiple_of(ka * rows + part * piece, 16), piece)]

    def hop(way, head, part):
        return remote(
            q_ref.at[pl.ds(part * piece, piece), columns(head)], query_part(z, core, part),
            hop_send.at[way, head, part], query_recv.at[z, core, part],
            pb=place + (n_y if way else -n_y), ka=head,
        )

    def hops(act):
        for part in range(cut):
            for way, there in ((0, hops_left), (1, hops_right)):
                @pl.when(there)
                def _():
                    for head in (core, other):
                        act(hop(way, head, part))

    def side_copy(which, head):
        source, target = ((k_ref, kbuf), (v_ref, vbuf))[which]
        return remote(
            source.at[:, columns(head)], target.at[y, my_rows],
            side_send.at[which, head], kv_recv.at[which, y, core], pb=across, ka=head,
        )

    def end_copy(which, head):
        source, target = ((k_ref, kend), (v_ref, vend))[which]
        return remote(
            source.at[:, columns(head)], target.at[y, my_rows],
            end_send.at[which, head], end_recv.at[which, y, core], pb=inner, ka=head,
        )

    def end_pass(which, ka):
        ref = (kend, vend)[which].at[y, rows_of(ka)]
        return remote(ref, ref, end_send.at[which, ka], end_recv.at[which, y, ka], pb=across)

    def wait_end(which, side, ka):
        ref = (kend, vend)[which].at[side, rows_of(ka)]
        remote(ref, ref, end_send.at[which, ka], end_recv.at[which, side, ka], pb=across).wait_recv()

    def pass_end(which):
        @pl.when(by_end)
        def _():
            for ka in (core, other):
                wait_end(which, y, ka)
                end_pass(which, ka).start()

    def swap(which):
        source, target = (
            (k_ref, kbuf.at[y, my_rows]), (v_ref, vbuf.at[y, my_rows]), (q_ref, qbuf.at[z, my_rows]),
        )[which]
        recv = query_recv.at[z, core, 0] if which == 2 else kv_recv.at[which, y, core]
        return remote(
            source.at[:, columns(other)], target, swap_send.at[which], recv, ka=other,
        )

    def code_hop(way):
        return remote(
            pairs_ref.at[core], codes.at[z], code_send.at[z, way], code_recv.at[z],
            pb=place + (n_y if way else -n_y),
        )

    def code_hops(act):
        for way, there in ((0, hops_left), (1, hops_right)):
            @pl.when(there)
            def _():
                act(code_hop(way))

    hops(lambda item: item.start())
    for which in range(2):
        for head in (core, other):
            side_copy(which, head).start()
    for which in (0, 2, 1):
        swap(which).start()
    code_hops(lambda item: item.start())

    @pl.when(at_end)
    def _():
        for which in range(2):
            for head in (core, other):
                end_copy(which, head).start()


    def wait_kv(which, side, ka):
        target = (kbuf, vbuf)[which].at[side, rows_of(ka)]
        remote(target, target, side_send.at[which, 0], kv_recv.at[which, side, ka], ka=other).wait_recv()

    row = lax.broadcasted_iota(jnp.int32, (STATS, tile), 0)
    shards = pairs_ref.shape[3]
    def pick_of(owner):
        pick = (
            lax.broadcasted_iota(jnp.int32, (STATS, shards), 1)
            == lax.broadcasted_iota(jnp.int32, (STATS, shards), 0) // blocks + owner * n_y * n_ka
        )
        return jnp.where(pick, 1.0, 0.0).astype(jnp.bfloat16)

    mine = pick_of(z)
    wanted = lax.broadcasted_iota(jnp.int32, (STATS, tile), 1) // BLOCK * blocks + row % blocks
    wanted = wanted.astype(jnp.float32)

    def mask(layer, listed, pick, start):
        spread = lax.dot_general(
            pick, listed.astype(jnp.float32).astype(jnp.bfloat16), (((1,), (1,)), ((), ())),
            preferred_element_type=jnp.float32,
        )
        hit = None
        for slot in range(listed.shape[0]):
            same = jnp.broadcast_to(spread[:, slot : slot + 1], (STATS, tile)) == wanted
            hit = same if hit is None else hit | same
        qturned[layer, pl.ds(start, STATS), :] = jnp.where(hit, 0.0, NEGATIVE_FILL).astype(qturned.dtype)

    def prepare(layer, listed):
        mask(layer, listed, mine, HEAD)
        qturned[layer, pl.ds(0, HEAD), :] = qbuf[layer].T

    def scores_of(layer, side):
        keys = jnp.concatenate([kbuf[side], marks[0, side]], axis=1)
        return dot(keys, qturned[layer])

    def first_half(layer):
        scores = scores_of(layer, y)
        top = scores.max(0, keepdims=True)
        chances = jnp.exp2((scores - top) * EXP2_SCALE)
        peak[layer] = top
        total[layer] = chances.sum(0, keepdims=True)
        accum[layer] = dot(vturned[y], chances.astype(jnp.bfloat16))

    stat_row = lax.broadcasted_iota(jnp.int32, (STATS, BLOCK), 0)

    def put_piece(layer, ka, top, whole, mixed):
        mixed = mixed * (1.0 / whole)
        ref = osend.at[layer, ka]
        for index in range(blocks):
            ref[pl.ds(index * HEAD, HEAD), :] = mixed[:, index * BLOCK : (index + 1) * BLOCK].astype(osend.dtype)
        put_level(ref, top * EXP2_SCALE + jnp.log2(whole))

    def put(layer, top, whole, mixed):
        for ka in range(n_ka):
            span = slice(ka * rows, (ka + 1) * rows)
            put_piece(layer, ka, top[:, span], whole[:, span], mixed[:, span])

    def second_state(layer):
        scores = scores_of(layer, far_y)
        before = peak[layer]
        top = jnp.maximum(before, scores.max(0, keepdims=True))
        rescale = jnp.exp2((before - top) * EXP2_SCALE)
        chances = jnp.exp2((scores - top) * EXP2_SCALE)
        whole = total[layer] * rescale + chances.sum(0, keepdims=True)
        return top, whole, accum[layer] * rescale + dot(vturned[far_y], chances.astype(jnp.bfloat16))

    def second_half(layer):
        put(layer, *second_state(layer))

    def whole_tile(layer, keys, hints, columns_of, start=0, size=tile):
        keys = jnp.concatenate([keys[...], hints[...]], axis=2).reshape(n_y * tile, 2 * HEAD)
        scores = dot(keys, qturned[layer, :, pl.ds(start, size)])
        top = scores.max(0, keepdims=True)
        chances = jnp.exp2((scores - top) * EXP2_SCALE)
        whole = chances.sum(0, keepdims=True)
        chances = chances.astype(jnp.bfloat16)
        mixed = dot(columns_of(0), chances[:tile])
        for side in range(1, n_y):
            mixed = mixed + dot(columns_of(side), chances[side * tile : (side + 1) * tile])
        return top, whole, mixed

    def both_halves(layer):
        for ka in range(n_ka):
            result = whole_tile(layer, kbuf, marks.at[0], lambda side: vturned[side], ka * rows, rows)
            put_piece(layer, ka, *result)
            give(layer, ka)

    def end_tile():
        top, whole, mixed = whole_tile(z, kend, marks.at[1], lambda side: vend[side].T)
        before = peak[z]
        after = jnp.maximum(before, top)
        old, new = jnp.exp2((before - after) * EXP2_SCALE), jnp.exp2((top - after) * EXP2_SCALE)
        put(z, after, total[z] * old + whole * new, accum[z] * old + mixed * new)

    def put_level(ref, level):
        high = level.astype(jnp.bfloat16).astype(jnp.float32)
        middle = (level - high).astype(jnp.bfloat16).astype(jnp.float32)
        low = level - high - middle
        stats = jnp.zeros((STATS, BLOCK), jnp.float32)
        for index in range(blocks):
            for order, term in enumerate((high, middle, low)):
                stats = jnp.where(stat_row == 3 * index + order, term[:, index * BLOCK : (index + 1) * BLOCK], stats)
        ref[pl.ds(blocks * HEAD, STATS), :] = stats.astype(ref.dtype)

    def level_of(ref):
        stats = ref[pl.ds(blocks * HEAD, STATS), :].astype(jnp.float32)
        levels = [stats[3 * i : 3 * i + 1] + stats[3 * i + 1 : 3 * i + 2] + stats[3 * i + 2 : 3 * i + 3] for i in range(blocks)]
        return jnp.concatenate(levels, axis=1)

    def blend(refs):
        levels = [level_of(ref) for ref in refs]
        top = functools.reduce(jnp.maximum, levels)
        shares = [jnp.exp2(level - top) for level in levels]
        whole = functools.reduce(jnp.add, shares)
        scale = 1.0 / whole
        shares = [share * scale for share in shares]
        mixed = []
        for index in range(blocks):
            span = slice(index * BLOCK, (index + 1) * BLOCK)
            terms = [ref[pl.ds(index * HEAD, HEAD), :].astype(jnp.float32) * share[:, span] for ref, share in zip(refs, shares)]
            mixed.append(functools.reduce(jnp.add, terms))
        return mixed, top + jnp.log2(whole)

    def merge(into, ref):
        mixed, level = blend((into, ref))
        for index in range(blocks):
            into[pl.ds(index * HEAD, HEAD), :] = mixed[index].astype(into.dtype)
        put_level(into, level)

    def straight(layer, ka):
        return remote(
            osend.at[layer, ka], orecv.at[z, core], out_send.at[layer, ka], out_recv.at[z, core],
            pb=layer * n_y + y, ka=ka,
        )

    def between(layer, ka):
        side = jnp.where(layer < z, 0, 1)
        return remote(
            osend.at[layer, ka], mrecv.at[side, ka], out_send.at[layer, ka], merge_recv.at[side, ka],
            pb=jnp.where(layer < z, place - n_y, place + n_y),
        )

    def two_away(layer):
        return jnp.logical_or(layer == z + 2, layer == z - 2)

    def give(layer, ka):
        @pl.when(two_away(layer))
        def _():
            between(layer, ka).start()

        @pl.when(jnp.logical_not(two_away(layer)))
        def _():
            straight(layer, ka).start()

    def give_other():
        return remote(
            osend.at[z, other], orecv.at[z, core], out_send.at[z, other], out_recv.at[z, core], ka=other,
        )

    shorter = jnp.minimum(z, n_z - 1 - z)
    long_right = z < n_z - 1 - z

    def layer_at(turn):
        both = turn <= 2 * shorter
        away = jnp.where(both, (turn + 1) // 2, turn - shorter)
        longer = jnp.where(both, turn % 2, 1)
        step = away * (2 * longer - 1)
        return jnp.where(long_right, z + step, z - step)

    def onward(layer):
        return jnp.logical_or(
            jnp.logical_and(layer < z, has_right), jnp.logical_and(layer > z, has_left)
        )

    def forward(layer, ka, part):
        ref = query_part(layer, ka, part)
        return remote(
            ref, ref, query_send.at[layer, ka, part], query_recv.at[layer, ka, part],
            pb=jnp.where(layer < z, place + n_y, place - n_y),
        )

    def code_forward(layer):
        return remote(
            codes.at[layer], codes.at[layer], code_send.at[layer, 0], code_recv.at[layer],
            pb=jnp.where(layer < z, place + n_y, place - n_y),
        )

    def take(layer, parts=tuple(range(cut))):
        for part in parts:
            for ka in (core, other):
                forward(layer, ka, part).wait_recv()

                @pl.when(onward(layer))
                def _():
                    forward(layer, ka, part).start()

            if part == 0:
                code_forward(layer).wait_recv()

                @pl.when(onward(layer))
                def _():
                    code_forward(layer).start()

    def ready(layer):
        prepare(layer, codes[layer, :, 0, :])

    for item in stage:
        item.wait()
    wait_kv(0, y, other)
    incoming = qbuf.at[z, other_rows]
    remote(incoming, incoming, swap_send.at[2], query_recv.at[z, other, 0], ka=other).wait_recv()
    prepare(z, pairs_ref[core, :, 0, :])
    wait_kv(1, y, other)
    vturned[y] = vbuf[y].T
    first_half(z)

    middle = jnp.logical_not(at_end)
    one, two, three = layer_at(1), layer_at(2), layer_at(3)

    @pl.when(middle)
    def _():
        take(one)
        take(two)
        ready(one)
        first_half(one)
        take(three, (0,))
        ready(two)
        first_half(two)
        take(three, tuple(range(1, cut)))
        ready(three)

    @pl.when(at_end)
    def _():
        take(two)
        ready(two)
        first_half(two)

    pass_end(0)
    for which in range(2):
        for ka in range(n_ka):
            wait_kv(which, far_y, ka)
    vturned[far_y] = vbuf[far_y].T

    def give_all(layer):
        for ka in (core, other):
            give(layer, ka)

    @pl.when(middle)
    def _():
        both_halves(three)
        second_half(one)
        pass_end(1)
        second_half(two)

    @pl.when(at_end)
    def _():
        second_half(two)
        give_all(two)
        take(three)
        ready(three)
        both_halves(three)

    late = jnp.where(at_end, three, two)
    final = jnp.where(by_end, one, late)

    if n_z > 4:
        def visit(turn, carry):
            layer = layer_at(turn)
            take(layer)
            ready(layer)
            both_halves(layer)
            return carry

        lax.fori_loop(4, n_z, visit, 0)

    @pl.when(jnp.logical_not(by_end))
    def _():
        second_half(z)
        give_other().start()

    @pl.when(by_end)
    def _():
        peak[z], total[z], accum[z] = second_state(z)

    @pl.when(middle)
    def _():
        for layer in (one, two):
            side = jnp.where(layer < z, 0, 1)
            for ka in range(n_ka):
                ref = mrecv.at[side, ka]
                remote(ref, ref, out_send.at[layer, ka], merge_recv.at[side, ka], ka=other).wait_recv()
                merge(osend.at[layer, ka], ref)
                straight(layer, ka).start()

    @pl.when(by_end)
    def _():
        mask(z, pairs_ref[core, :, 0, :], pick_of(last), HEAD + STATS)
        for which in range(2):
            for ka in range(n_ka):
                wait_end(which, far_y, ka)
        end_tile()
        give_other().start()

    def wait_out(layer, head):
        ref = orecv.at[layer, head]
        remote(ref, ref, out_send.at[z, 0], out_recv.at[layer, head], ka=other).wait_recv()

    wait_out(z, other)
    if n_z > 4:
        def gather(turn, carry):
            layer = layer_at(turn)

            @pl.when(jnp.logical_not(two_away(layer)))
            def _():
                for head in (core, other):
                    wait_out(layer, head)
                merge(osend.at[z, core], orecv.at[layer, core])
                merge(orecv.at[z, other], orecv.at[layer, other])

            return carry

        lax.fori_loop(4, n_z, gather, 0)
    @pl.when(jnp.logical_not(by_end))
    def _():
        for head in (core, other):
            wait_out(one, head)
        merge(osend.at[z, core], orecv.at[one, core])
        merge(orecv.at[z, other], orecv.at[one, other])

    keeps = []
    for index, head in enumerate((core, other)):
        wait_out(final, head)
        refs = [orecv.at[z, head] if index else osend.at[z, core], orecv.at[final, head]]
        for block, mixed in enumerate(blend(refs)[0]):
            obuf[index, pl.ds(block * BLOCK, BLOCK), :] = mixed.T.astype(obuf.dtype)
        keep = pltpu.make_async_copy(obuf.at[index], out_ref.at[:, columns(head)], local_sem.at[3 + index])
        keep.start()
        keeps.append(keep)

    hops(lambda item: item.wait_send())
    for which in range(2):
        for head in range(n_ka):
            side_copy(which, head).wait_send()
    for which in range(3):
        swap(which).wait_send()
    code_hops(lambda item: item.wait_send())

    def drain(turn, carry):
        layer = layer_at(turn)

        @pl.when(jnp.logical_or(middle, turn != 1))
        def _():
            for ka in range(n_ka):
                straight(layer, ka).wait_send()

        @pl.when(onward(layer))
        def _():
            code_forward(layer).wait_send()
            for ka in range(n_ka):
                for part in range(cut):
                    forward(layer, ka, part).wait_send()

        return carry

    lax.fori_loop(1, n_z, drain, 0)

    @pl.when(at_end)
    def _():
        for which in range(2):
            for head in range(n_ka):
                end_copy(which, head).wait_send()

    @pl.when(by_end)
    def _():
        for which in range(2):
            for ka in range(n_ka):
                end_pass(which, ka).wait_send()

    give_other().wait_send()
    for keep in keeps:
        keep.wait()


def solution(mesh):
    n_pb, n_ka = mesh.shape["pb"], mesh.shape["ka"]
    width = 2
    cut = 2

    def local(queries, keys, values, block_pairs):
        rows = queries.shape[0]
        tile = n_ka * rows
        shards, most = block_pairs.shape[2:]
        n_z = n_pb // width
        anywhere = pl.BlockSpec(memory_space=pl.ANY)
        half = jnp.bfloat16
        dma = pltpu.SemaphoreType.DMA
        return pl.pallas_call(
            functools.partial(kernel, n_pb, n_ka, width, cut),
            out_shape=jax.ShapeDtypeStruct(queries.shape, queries.dtype),
            in_specs=[anywhere, anywhere, anywhere, pl.BlockSpec(memory_space=pltpu.VMEM)],
            out_specs=anywhere,
            scratch_shapes=[
                pltpu.VMEM((n_z, tile, HEAD), half),
                pltpu.VMEM((width, tile, HEAD), half),
                pltpu.VMEM((width, tile, HEAD), half),
                pltpu.VMEM((width, tile, HEAD), half),
                pltpu.VMEM((width, tile, HEAD), half),
                pltpu.VMEM((n_z, most, 1, shards), jnp.int32),
                pltpu.VMEM((2, width, tile, HEAD), half),
                pltpu.VMEM((n_z, 2 * HEAD, tile), half),
                pltpu.VMEM((width, HEAD, tile), half),
                pltpu.VMEM((n_z, 1, tile), jnp.float32),
                pltpu.VMEM((n_z, 1, tile), jnp.float32),
                pltpu.VMEM((n_z, HEAD, tile), jnp.float32),
                pltpu.VMEM((n_z, n_ka, rows + STATS, HEAD), half),
                pltpu.VMEM((n_z, n_ka, rows + STATS, HEAD), half),
                pltpu.VMEM((2, n_ka, rows + STATS, HEAD), half),
                pltpu.VMEM((n_ka, rows, HEAD), half),
                dma((2, n_ka, cut)),
                dma((n_z, n_ka, cut)),
                dma((n_z, n_ka, cut)),
                dma((n_z, 2)),
                dma((n_z,)),
                dma((2, n_ka)),
                dma((2, width, n_ka)),
                dma((3,)),
                dma((n_z, n_ka)),
                dma((n_z, n_ka)),
                dma((2, n_ka)),
                dma((2, n_ka)),
                dma((2, width, n_ka)),
                dma((5,)),
            ],
            compiler_params=pltpu.CompilerParams(
                collective_id=0, has_side_effects=True, vmem_limit_bytes=56 * 1024 * 1024
            ),
        )(queries, keys, values, block_pairs.transpose(0, 3, 1, 2))

    rows_spec = P(("groups", "pb", "ka"), None)
    return jax.shard_map(
        local, mesh=mesh,
        in_specs=(rows_spec, rows_spec, rows_spec, P("groups", "pb", None, None)),
        out_specs=rows_spec, check_vma=False,
    )
```

```python
import functools
import math

import jax
import jax.numpy as jnp
from jax import lax
from jax.experimental import pallas as pl
from jax.experimental.pallas import tpu as pltpu
from jax.sharding import PartitionSpec as P

HEAD = 128
BLOCK = 128
STATS = 16
NEGATIVE_FILL = -1e30
EXP2_SCALE = HEAD ** (-0.5) * math.log2(math.e)
MESH = pl.DeviceIdType.MESH


def dot(a, b):
    return lax.dot_general(a, b, (((1,), (0,)), ((), ())), preferred_element_type=jnp.float32)


def kernel(
    n_pb, n_ka, width, cut, q_ref, k_ref, v_ref, pairs_ref, out_ref,
    qbuf, kbuf, vbuf, kend, vend, codes, marks, qturned, vturned, peak, total, accum, osend, orecv, mrecv, obuf,
    hop_send, query_send, query_recv, code_send, code_recv, side_send, kv_recv,
    swap_send, out_send, out_recv, merge_recv, end_send, end_recv, local_sem,
):
    rows = q_ref.shape[0]
    tile = n_ka * rows
    blocks = rows // BLOCK
    n_y = width
    n_z = n_pb // n_y
    core = lax.axis_index("ka")
    place = lax.axis_index("pb")
    z, y = place // n_y, place % n_y
    other = 1 - core
    far_y = 1 - y
    across = z * n_y + far_y
    has_left, has_right = z > 0, z < n_z - 1
    piece = rows // cut

    barrier = pltpu.get_barrier_semaphore()

    def greet(pb, ka):
        pl.semaphore_signal(barrier, inc=1, device_id={"pb": pb, "ka": ka}, device_id_type=MESH)

    at_end = jnp.logical_not(jnp.logical_and(has_left, has_right))
    by_end = jnp.logical_or(z == 1, z == n_z - 2)
    last = jnp.where(z < n_z - 1 - z, 0, n_z - 1)
    inner = jnp.where(has_left, place - n_y, place + n_y)
    hops_left, hops_right = z > 1, z < n_z - 2
    hops_left = jnp.logical_or(hops_left, z == n_z - 1)
    hops_right = jnp.logical_or(hops_right, z == 0)
    for ka in range(n_ka):
        @pl.when(has_left)
        def _():
            greet(place - n_y, ka)

        @pl.when(has_right)
        def _():
            greet(place + n_y, ka)

        greet(across, ka)
    greet(place, other)

    def columns(head):
        return pl.ds(pl.multiple_of(head * HEAD, HEAD), HEAD)

    def rows_of(ka):
        return pl.ds(pl.multiple_of(ka * rows, BLOCK), rows)

    my_rows, other_rows = rows_of(core), rows_of(other)

    stage = [
        pltpu.make_async_copy(k_ref.at[:, columns(core)], kbuf.at[y, my_rows], local_sem.at[0]),
        pltpu.make_async_copy(q_ref.at[:, columns(core)], qbuf.at[z, my_rows], local_sem.at[1]),
        pltpu.make_async_copy(v_ref.at[:, columns(core)], vbuf.at[y, my_rows], local_sem.at[2]),
    ]
    for item in stage:
        item.start()

    def remote(source, target, send_sem, recv_sem, **device):
        return pltpu.make_async_remote_copy(
            src_ref=source, dst_ref=target, send_sem=send_sem, recv_sem=recv_sem,
            device_id=device, device_id_type=MESH,
        )

    block_of_row = lax.broadcasted_iota(jnp.int32, (tile, HEAD), 0) // BLOCK
    lane = lax.broadcasted_iota(jnp.int32, (tile, HEAD), 1)
    for side in range(n_y):
        here = lane == block_of_row + side * n_ka * blocks
        marks[0, side] = jnp.where(here, 1.0, 0.0).astype(marks.dtype)
        there = lane == block_of_row + side * n_ka * blocks + STATS
        marks[1, side] = jnp.where(there, 1.0, 0.0).astype(marks.dtype)
    pad = qturned.shape[1] - HEAD - STATS
    for layer in range(n_z):
        qturned[layer, pl.ds(HEAD + STATS, pad), :] = jnp.zeros((pad, tile), qturned.dtype)

    beside = has_left.astype(jnp.int32) + has_right.astype(jnp.int32)
    pl.semaphore_wait(barrier, n_ka * (1 + beside) + 1)

    def query_part(layer, ka, part):
        return qbuf.at[layer, pl.ds(pl.multiple_of(ka * rows + part * piece, 16), piece)]

    def hop(way, head, part):
        return remote(
            q_ref.at[pl.ds(part * piece, piece), columns(head)], query_part(z, core, part),
            hop_send.at[way, head, part], query_recv.at[z, core, part],
            pb=place + (n_y if way else -n_y), ka=head,
        )

    def hops(act):
        for part in range(cut):
            for way, there in ((0, hops_left), (1, hops_right)):
                @pl.when(there)
                def _():
                    for head in (core, other):
                        act(hop(way, head, part))

    def side_copy(which, head):
        source, target = ((k_ref, kbuf), (v_ref, vbuf))[which]
        return remote(
            source.at[:, columns(head)], target.at[y, my_rows],
            side_send.at[which, head], kv_recv.at[which, y, core], pb=across, ka=head,
        )

    def end_copy(which, head):
        source, target = ((k_ref, kend), (v_ref, vend))[which]
        return remote(
            source.at[:, columns(head)], target.at[y, my_rows],
            end_send.at[which, head], end_recv.at[which, y, core], pb=inner, ka=head,
        )

    def end_pass(which, ka):
        ref = (kend, vend)[which].at[y, rows_of(ka)]
        return remote(ref, ref, end_send.at[which, ka], end_recv.at[which, y, ka], pb=across)

    def wait_end(which, side, ka):
        ref = (kend, vend)[which].at[side, rows_of(ka)]
        remote(ref, ref, end_send.at[which, ka], end_recv.at[which, side, ka], pb=across).wait_recv()

    def pass_end(which):
        @pl.when(by_end)
        def _():
            for ka in (core, other):
                wait_end(which, y, ka)
                end_pass(which, ka).start()

    def swap(which):
        source, target = (
            (k_ref, kbuf.at[y, my_rows]), (v_ref, vbuf.at[y, my_rows]), (q_ref, qbuf.at[z, my_rows]),
        )[which]
        recv = query_recv.at[z, core, 0] if which == 2 else kv_recv.at[which, y, core]
        return remote(
            source.at[:, columns(other)], target, swap_send.at[which], recv, ka=other,
        )

    def code_hop(way):
        return remote(
            pairs_ref.at[core], codes.at[z], code_send.at[z, way], code_recv.at[z],
            pb=place + (n_y if way else -n_y),
        )

    def code_hops(act):
        for way, there in ((0, hops_left), (1, hops_right)):
            @pl.when(there)
            def _():
                act(code_hop(way))

    hops(lambda item: item.start())
    for which in range(2):
        for head in (core, other):
            side_copy(which, head).start()
    for which in (0, 2, 1):
        swap(which).start()
    code_hops(lambda item: item.start())

    @pl.when(at_end)
    def _():
        for which in range(2):
            for head in (core, other):
                end_copy(which, head).start()


    def wait_kv(which, side, ka):
        target = (kbuf, vbuf)[which].at[side, rows_of(ka)]
        remote(target, target, side_send.at[which, 0], kv_recv.at[which, side, ka], ka=other).wait_recv()

    row = lax.broadcasted_iota(jnp.int32, (STATS, tile), 0)
    shards = pairs_ref.shape[3]
    def pick_of(owner):
        pick = (
            lax.broadcasted_iota(jnp.int32, (STATS, shards), 1)
            == lax.broadcasted_iota(jnp.int32, (STATS, shards), 0) // blocks + owner * n_y * n_ka
        )
        return jnp.where(pick, 1.0, 0.0).astype(jnp.bfloat16)

    mine = pick_of(z)
    wanted = lax.broadcasted_iota(jnp.int32, (STATS, tile), 1) // BLOCK * blocks + row % blocks
    wanted = wanted.astype(jnp.float32)

    def mask(layer, listed, pick, start):
        spread = lax.dot_general(
            pick, listed.astype(jnp.float32).astype(jnp.bfloat16), (((1,), (1,)), ((), ())),
            preferred_element_type=jnp.float32,
        )
        hit = None
        for slot in range(listed.shape[0]):
            same = jnp.broadcast_to(spread[:, slot : slot + 1], (STATS, tile)) == wanted
            hit = same if hit is None else hit | same
        qturned[layer, pl.ds(start, STATS), :] = jnp.where(hit, 0.0, NEGATIVE_FILL).astype(qturned.dtype)

    def prepare(layer, listed):
        mask(layer, listed, mine, HEAD)
        qturned[layer, pl.ds(0, HEAD), :] = qbuf[layer].T

    def scores_of(layer, side):
        keys = jnp.concatenate([kbuf[side], marks[0, side]], axis=1)
        return dot(keys, qturned[layer])

    def first_half(layer):
        scores = scores_of(layer, y)
        top = scores.max(0, keepdims=True)
        chances = jnp.exp2((scores - top) * EXP2_SCALE)
        peak[layer] = top
        total[layer] = chances.sum(0, keepdims=True)
        accum[layer] = dot(vturned[y], chances.astype(jnp.bfloat16))

    stat_row = lax.broadcasted_iota(jnp.int32, (STATS, BLOCK), 0)

    def put_piece(layer, ka, top, whole, mixed):
        mixed = mixed * (1.0 / whole)
        ref = osend.at[layer, ka]
        for index in range(blocks):
            ref[pl.ds(index * HEAD, HEAD), :] = mixed[:, index * BLOCK : (index + 1) * BLOCK].astype(osend.dtype)
        put_level(ref, top * EXP2_SCALE + jnp.log2(whole))

    def put(layer, top, whole, mixed):
        for ka in range(n_ka):
            span = slice(ka * rows, (ka + 1) * rows)
            put_piece(layer, ka, top[:, span], whole[:, span], mixed[:, span])

    def second_state(layer):
        scores = scores_of(layer, far_y)
        before = peak[layer]
        top = jnp.maximum(before, scores.max(0, keepdims=True))
        rescale = jnp.exp2((before - top) * EXP2_SCALE)
        chances = jnp.exp2((scores - top) * EXP2_SCALE)
        whole = total[layer] * rescale + chances.sum(0, keepdims=True)
        return top, whole, accum[layer] * rescale + dot(vturned[far_y], chances.astype(jnp.bfloat16))

    def second_half(layer):
        put(layer, *second_state(layer))

    def whole_tile(layer, keys, hints, columns_of, start=0, size=tile):
        keys = jnp.concatenate([keys[...], hints[...]], axis=2).reshape(n_y * tile, 2 * HEAD)
        scores = dot(keys, qturned[layer, :, pl.ds(start, size)])
        top = scores.max(0, keepdims=True)
        chances = jnp.exp2((scores - top) * EXP2_SCALE)
        whole = chances.sum(0, keepdims=True)
        chances = chances.astype(jnp.bfloat16)
        mixed = dot(columns_of(0), chances[:tile])
        for side in range(1, n_y):
            mixed = mixed + dot(columns_of(side), chances[side * tile : (side + 1) * tile])
        return top, whole, mixed

    def both_halves(layer):
        for ka in (core, other):
            result = whole_tile(layer, kbuf, marks.at[0], lambda side: vturned[side], pl.multiple_of(ka * rows, BLOCK), rows)
            put_piece(layer, ka, *result)
            give(layer, ka)

    def end_tile():
        top, whole, mixed = whole_tile(z, kend, marks.at[1], lambda side: vend[side].T)
        before = peak[z]
        after = jnp.maximum(before, top)
        old, new = jnp.exp2((before - after) * EXP2_SCALE), jnp.exp2((top - after) * EXP2_SCALE)
        put(z, after, total[z] * old + whole * new, accum[z] * old + mixed * new)

    def put_level(ref, level):
        high = level.astype(jnp.bfloat16).astype(jnp.float32)
        middle = (level - high).astype(jnp.bfloat16).astype(jnp.float32)
        low = level - high - middle
        stats = jnp.zeros((STATS, BLOCK), jnp.float32)
        for index in range(blocks):
            for order, term in enumerate((high, middle, low)):
                stats = jnp.where(stat_row == 3 * index + order, term[:, index * BLOCK : (index + 1) * BLOCK], stats)
        ref[pl.ds(blocks * HEAD, STATS), :] = stats.astype(ref.dtype)

    def level_of(ref):
        stats = ref[pl.ds(blocks * HEAD, STATS), :].astype(jnp.float32)
        levels = [stats[3 * i : 3 * i + 1] + stats[3 * i + 1 : 3 * i + 2] + stats[3 * i + 2 : 3 * i + 3] for i in range(blocks)]
        return jnp.concatenate(levels, axis=1)

    def blend(refs):
        levels = [level_of(ref) for ref in refs]
        top = functools.reduce(jnp.maximum, levels)
        shares = [jnp.exp2(level - top) for level in levels]
        whole = functools.reduce(jnp.add, shares)
        scale = 1.0 / whole
        shares = [share * scale for share in shares]
        mixed = []
        for index in range(blocks):
            span = slice(index * BLOCK, (index + 1) * BLOCK)
            terms = [ref[pl.ds(index * HEAD, HEAD), :].astype(jnp.float32) * share[:, span] for ref, share in zip(refs, shares)]
            mixed.append(functools.reduce(jnp.add, terms))
        return mixed, top + jnp.log2(whole)

    def merge(into, ref):
        mixed, level = blend((into, ref))
        for index in range(blocks):
            into[pl.ds(index * HEAD, HEAD), :] = mixed[index].astype(into.dtype)
        put_level(into, level)

    def straight(layer, ka):
        return remote(
            osend.at[layer, ka], orecv.at[z, core], out_send.at[layer, ka], out_recv.at[z, core],
            pb=layer * n_y + y, ka=ka,
        )

    def between(layer, ka):
        side = jnp.where(layer < z, 0, 1)
        return remote(
            osend.at[layer, ka], mrecv.at[side, ka], out_send.at[layer, ka], merge_recv.at[side, ka],
            pb=jnp.where(layer < z, place - n_y, place + n_y),
        )

    def two_away(layer):
        return jnp.logical_or(layer == z + 2, layer == z - 2)

    def is_end(layer):
        return jnp.logical_or(layer == 0, layer == n_z - 1)

    def merges(layer, ka):
        return jnp.logical_and(two_away(layer), jnp.logical_or(ka != core, jnp.logical_not(is_end(layer))))

    def give(layer, ka):
        @pl.when(merges(layer, ka))
        def _():
            between(layer, ka).start()

        @pl.when(jnp.logical_not(merges(layer, ka)))
        def _():
            straight(layer, ka).start()

    def give_other():
        return remote(
            osend.at[z, other], orecv.at[z, core], out_send.at[z, other], out_recv.at[z, core], ka=other,
        )

    shorter = jnp.minimum(z, n_z - 1 - z)
    long_right = z < n_z - 1 - z

    def layer_at(turn):
        both = turn <= 2 * shorter
        away = jnp.where(both, (turn + 1) // 2, turn - shorter)
        longer = jnp.where(both, turn % 2, 1)
        step = away * (2 * longer - 1)
        return jnp.where(long_right, z + step, z - step)

    def onward(layer):
        return jnp.logical_or(
            jnp.logical_and(layer < z, has_right), jnp.logical_and(layer > z, has_left)
        )

    def forward(layer, ka, part):
        ref = query_part(layer, ka, part)
        return remote(
            ref, ref, query_send.at[layer, ka, part], query_recv.at[layer, ka, part],
            pb=jnp.where(layer < z, place + n_y, place - n_y),
        )

    def code_forward(layer):
        return remote(
            codes.at[layer], codes.at[layer], code_send.at[layer, 0], code_recv.at[layer],
            pb=jnp.where(layer < z, place + n_y, place - n_y),
        )

    def take(layer, parts=tuple(range(cut))):
        for part in parts:
            for ka in (core, other):
                forward(layer, ka, part).wait_recv()

                @pl.when(onward(layer))
                def _():
                    forward(layer, ka, part).start()

            if part == 0:
                code_forward(layer).wait_recv()

                @pl.when(onward(layer))
                def _():
                    code_forward(layer).start()

    def ready(layer):
        prepare(layer, codes[layer, :, 0, :])

    for item in stage:
        item.wait()
    wait_kv(0, y, other)
    incoming = qbuf.at[z, other_rows]
    remote(incoming, incoming, swap_send.at[2], query_recv.at[z, other, 0], ka=other).wait_recv()
    prepare(z, pairs_ref[core, :, 0, :])
    wait_kv(1, y, other)
    vturned[y] = vbuf[y].T
    first_half(z)

    middle = jnp.logical_not(at_end)
    one, two, three = layer_at(1), layer_at(2), layer_at(3)

    @pl.when(middle)
    def _():
        take(one)
        take(two)
        ready(one)
        first_half(one)
        take(three, (0,))
        ready(two)
        first_half(two)
        take(three, tuple(range(1, cut)))
        ready(three)

    @pl.when(at_end)
    def _():
        take(two)
        ready(two)
        first_half(two)

    pass_end(0)
    for which in range(2):
        for ka in range(n_ka):
            wait_kv(which, far_y, ka)
    vturned[far_y] = vbuf[far_y].T

    def give_all(layer):
        for ka in (core, other):
            give(layer, ka)

    @pl.when(middle)
    def _():
        both_halves(three)
        second_half(two)

        @pl.when(by_end)
        def _():
            straight(two, core).start()

        second_half(one)
        pass_end(1)

    @pl.when(at_end)
    def _():
        second_half(two)
        give_all(two)
        take(three)
        ready(three)
        both_halves(three)

    late = jnp.where(at_end, three, two)
    final = jnp.where(by_end, one, late)

    if n_z > 4:
        def visit(turn, carry):
            layer = layer_at(turn)
            take(layer)
            ready(layer)
            both_halves(layer)
            return carry

        lax.fori_loop(4, n_z, visit, 0)

    @pl.when(jnp.logical_not(by_end))
    def _():
        second_half(z)
        give_other().start()

    @pl.when(by_end)
    def _():
        peak[z], total[z], accum[z] = second_state(z)

    @pl.when(middle)
    def _():
        for layer in (two, one):
            side = jnp.where(layer < z, 0, 1)
            for ka in range(n_ka):
                @pl.when(jnp.logical_or(ka != core, jnp.logical_not(is_end(layer))))
                def _(layer=layer, side=side, ka=ka):
                    ref = mrecv.at[side, ka]
                    remote(ref, ref, out_send.at[layer, ka], merge_recv.at[side, ka], ka=other).wait_recv()
                    merge(osend.at[layer, ka], ref)
                    straight(layer, ka).start()

    @pl.when(by_end)
    def _():
        mask(z, pairs_ref[core, :, 0, :], pick_of(last), HEAD + STATS)
        for which in range(2):
            for ka in range(n_ka):
                wait_end(which, far_y, ka)
        end_tile()
        give_other().start()

    def wait_out(layer, head):
        ref = orecv.at[layer, head]
        remote(ref, ref, out_send.at[z, 0], out_recv.at[layer, head], ka=other).wait_recv()

    wait_out(z, other)
    if n_z > 4:
        def gather(turn, carry):
            layer = layer_at(turn)

            @pl.when(jnp.logical_not(two_away(layer)))
            def _():
                for head in (core, other):
                    wait_out(layer, head)
                merge(osend.at[z, core], orecv.at[layer, core])
                merge(orecv.at[z, other], orecv.at[layer, other])

            return carry

        lax.fori_loop(4, n_z, gather, 0)
    @pl.when(jnp.logical_not(by_end))
    def _():
        for head in (core, other):
            wait_out(one, head)
        merge(osend.at[z, core], orecv.at[one, core])
        merge(orecv.at[z, other], orecv.at[one, other])

    @pl.when(at_end)
    def _():
        wait_out(two, core)
        merge(osend.at[z, core], orecv.at[two, core])

    keeps = []
    for index, head in enumerate((core, other)):
        wait_out(final, head)
        refs = [orecv.at[z, head] if index else osend.at[z, core], orecv.at[final, head]]
        for block, mixed in enumerate(blend(refs)[0]):
            obuf[index, pl.ds(block * BLOCK, BLOCK), :] = mixed.T.astype(obuf.dtype)
        keep = pltpu.make_async_copy(obuf.at[index], out_ref.at[:, columns(head)], local_sem.at[3 + index])
        keep.start()
        keeps.append(keep)

    hops(lambda item: item.wait_send())
    for which in range(2):
        for head in range(n_ka):
            side_copy(which, head).wait_send()
    for which in range(3):
        swap(which).wait_send()
    code_hops(lambda item: item.wait_send())

    def drain(turn, carry):
        layer = layer_at(turn)

        @pl.when(jnp.logical_or(middle, turn != 1))
        def _():
            for ka in range(n_ka):
                straight(layer, ka).wait_send()

        @pl.when(onward(layer))
        def _():
            code_forward(layer).wait_send()
            for ka in range(n_ka):
                for part in range(cut):
                    forward(layer, ka, part).wait_send()

        return carry

    lax.fori_loop(1, n_z, drain, 0)

    @pl.when(at_end)
    def _():
        for which in range(2):
            for head in range(n_ka):
                end_copy(which, head).wait_send()

    @pl.when(by_end)
    def _():
        for which in range(2):
            for ka in range(n_ka):
                end_pass(which, ka).wait_send()

    give_other().wait_send()
    for keep in keeps:
        keep.wait()


def solution(mesh):
    n_pb, n_ka = mesh.shape["pb"], mesh.shape["ka"]
    width = 2
    cut = 2

    def local(queries, keys, values, block_pairs):
        rows = queries.shape[0]
        tile = n_ka * rows
        shards, most = block_pairs.shape[2:]
        n_z = n_pb // width
        anywhere = pl.BlockSpec(memory_space=pl.ANY)
        half = jnp.bfloat16
        dma = pltpu.SemaphoreType.DMA
        return pl.pallas_call(
            functools.partial(kernel, n_pb, n_ka, width, cut),
            out_shape=jax.ShapeDtypeStruct(queries.shape, queries.dtype),
            in_specs=[anywhere, anywhere, anywhere, pl.BlockSpec(memory_space=pltpu.VMEM)],
            out_specs=anywhere,
            scratch_shapes=[
                pltpu.VMEM((n_z, tile, HEAD), half),
                pltpu.VMEM((width, tile, HEAD), half),
                pltpu.VMEM((width, tile, HEAD), half),
                pltpu.VMEM((width, tile, HEAD), half),
                pltpu.VMEM((width, tile, HEAD), half),
                pltpu.VMEM((n_z, most, 1, shards), jnp.int32),
                pltpu.VMEM((2, width, tile, HEAD), half),
                pltpu.VMEM((n_z, 2 * HEAD, tile), half),
                pltpu.VMEM((width, HEAD, tile), half),
                pltpu.VMEM((n_z, 1, tile), jnp.float32),
                pltpu.VMEM((n_z, 1, tile), jnp.float32),
                pltpu.VMEM((n_z, HEAD, tile), jnp.float32),
                pltpu.VMEM((n_z, n_ka, rows + STATS, HEAD), half),
                pltpu.VMEM((n_z, n_ka, rows + STATS, HEAD), half),
                pltpu.VMEM((2, n_ka, rows + STATS, HEAD), half),
                pltpu.VMEM((n_ka, rows, HEAD), half),
                dma((2, n_ka, cut)),
                dma((n_z, n_ka, cut)),
                dma((n_z, n_ka, cut)),
                dma((n_z, 2)),
                dma((n_z,)),
                dma((2, n_ka)),
                dma((2, width, n_ka)),
                dma((3,)),
                dma((n_z, n_ka)),
                dma((n_z, n_ka)),
                dma((2, n_ka)),
                dma((2, n_ka)),
                dma((2, width, n_ka)),
                dma((5,)),
            ],
            compiler_params=pltpu.CompilerParams(
                collective_id=0, has_side_effects=True, vmem_limit_bytes=56 * 1024 * 1024
            ),
        )(queries, keys, values, block_pairs.transpose(0, 3, 1, 2))

    rows_spec = P(("groups", "pb", "ka"), None)
    return jax.shard_map(
        local, mesh=mesh,
        in_specs=(rows_spec, rows_spec, rows_spec, P("groups", "pb", None, None)),
        out_specs=rows_spec, check_vma=False,
    )
```

```python
import functools
import math

import jax
import jax.numpy as jnp
from jax import lax
from jax.experimental import pallas as pl
from jax.experimental.pallas import tpu as pltpu
from jax.sharding import PartitionSpec as P

HEAD = 128
BLOCK = 128
STATS = 16
NEGATIVE_FILL = -1e30
EXP2_SCALE = HEAD ** (-0.5) * math.log2(math.e)
MESH = pl.DeviceIdType.MESH


def dot(a, b):
    return lax.dot_general(a, b, (((1,), (0,)), ((), ())), preferred_element_type=jnp.float32)


def kernel(
    n_pb, n_ka, width, cut, q_ref, k_ref, v_ref, pairs_ref, out_ref,
    qbuf, kbuf, vbuf, kend, vend, codes, marks, qturned, vturned, peak, total, accum, osend, orecv, mrecv, obuf,
    hop_send, query_send, query_recv, code_send, code_recv, side_send, kv_recv,
    swap_send, out_send, out_recv, merge_recv, end_send, end_recv, local_sem,
):
    rows = q_ref.shape[0]
    tile = n_ka * rows
    blocks = rows // BLOCK
    n_y = width
    n_z = n_pb // n_y
    core = lax.axis_index("ka")
    place = lax.axis_index("pb")
    z, y = place // n_y, place % n_y
    other = 1 - core
    far_y = 1 - y
    across = z * n_y + far_y
    has_left, has_right = z > 0, z < n_z - 1
    piece = rows // cut

    barrier = pltpu.get_barrier_semaphore()

    def greet(pb, ka):
        pl.semaphore_signal(barrier, inc=1, device_id={"pb": pb, "ka": ka}, device_id_type=MESH)

    at_end = jnp.logical_not(jnp.logical_and(has_left, has_right))
    by_end = jnp.logical_or(z == 1, z == n_z - 2)
    last = jnp.where(z < n_z - 1 - z, 0, n_z - 1)
    inner = jnp.where(has_left, place - n_y, place + n_y)
    hops_left, hops_right = z > 1, z < n_z - 2
    hops_left = jnp.logical_or(hops_left, z == n_z - 1)
    hops_right = jnp.logical_or(hops_right, z == 0)
    for ka in range(n_ka):
        @pl.when(has_left)
        def _():
            greet(place - n_y, ka)

        @pl.when(has_right)
        def _():
            greet(place + n_y, ka)

        greet(across, ka)
    greet(place, other)

    def columns(head):
        return pl.ds(pl.multiple_of(head * HEAD, HEAD), HEAD)

    def rows_of(ka):
        return pl.ds(pl.multiple_of(ka * rows, BLOCK), rows)

    my_rows, other_rows = rows_of(core), rows_of(other)

    stage = [
        pltpu.make_async_copy(k_ref.at[:, columns(core)], kbuf.at[y, my_rows], local_sem.at[0]),
        pltpu.make_async_copy(q_ref.at[:, columns(core)], qbuf.at[z, my_rows], local_sem.at[1]),
        pltpu.make_async_copy(v_ref.at[:, columns(core)], vbuf.at[y, my_rows], local_sem.at[2]),
    ]
    for item in stage:
        item.start()

    def remote(source, target, send_sem, recv_sem, **device):
        return pltpu.make_async_remote_copy(
            src_ref=source, dst_ref=target, send_sem=send_sem, recv_sem=recv_sem,
            device_id=device, device_id_type=MESH,
        )

    block_of_row = lax.broadcasted_iota(jnp.int32, (tile, HEAD), 0) // BLOCK
    lane = lax.broadcasted_iota(jnp.int32, (tile, HEAD), 1)
    for side in range(n_y):
        here = lane == block_of_row + side * n_ka * blocks
        marks[0, side] = jnp.where(here, 1.0, 0.0).astype(marks.dtype)
        there = lane == block_of_row + side * n_ka * blocks + STATS
        marks[1, side] = jnp.where(there, 1.0, 0.0).astype(marks.dtype)
    pad = qturned.shape[1] - HEAD - STATS
    for layer in range(n_z):
        qturned[layer, pl.ds(HEAD + STATS, pad), :] = jnp.zeros((pad, tile), qturned.dtype)

    beside = has_left.astype(jnp.int32) + has_right.astype(jnp.int32)
    pl.semaphore_wait(barrier, n_ka * (1 + beside) + 1)

    def query_part(layer, ka, part):
        return qbuf.at[layer, pl.ds(pl.multiple_of(ka * rows + part * piece, 16), piece)]

    def hop(way, head, part):
        return remote(
            q_ref.at[pl.ds(part * piece, piece), columns(head)], query_part(z, core, part),
            hop_send.at[way, head, part], query_recv.at[z, core, part],
            pb=place + (n_y if way else -n_y), ka=head,
        )

    def hops(act):
        for part in range(cut):
            for way, there in ((0, hops_left), (1, hops_right)):
                @pl.when(there)
                def _():
                    for head in (core, other):
                        act(hop(way, head, part))

    def side_copy(which, head):
        source, target = ((k_ref, kbuf), (v_ref, vbuf))[which]
        return remote(
            source.at[:, columns(head)], target.at[y, my_rows],
            side_send.at[which, head], kv_recv.at[which, y, core], pb=across, ka=head,
        )

    def end_copy(which, head):
        source, target = ((k_ref, kend), (v_ref, vend))[which]
        return remote(
            source.at[:, columns(head)], target.at[y, my_rows],
            end_send.at[which, head], end_recv.at[which, y, core], pb=inner, ka=head,
        )

    def end_pass(which, ka):
        ref = (kend, vend)[which].at[y, rows_of(ka)]
        return remote(ref, ref, end_send.at[which, ka], end_recv.at[which, y, ka], pb=across)

    def wait_end(which, side, ka):
        ref = (kend, vend)[which].at[side, rows_of(ka)]
        remote(ref, ref, end_send.at[which, ka], end_recv.at[which, side, ka], pb=across).wait_recv()

    def pass_end(which):
        @pl.when(by_end)
        def _():
            for ka in (core, other):
                wait_end(which, y, ka)
                end_pass(which, ka).start()

    def swap(which):
        source, target = (
            (k_ref, kbuf.at[y, my_rows]), (v_ref, vbuf.at[y, my_rows]), (q_ref, qbuf.at[z, my_rows]),
        )[which]
        recv = query_recv.at[z, core, 0] if which == 2 else kv_recv.at[which, y, core]
        return remote(
            source.at[:, columns(other)], target, swap_send.at[which], recv, ka=other,
        )

    def code_hop(way):
        return remote(
            pairs_ref.at[core], codes.at[z], code_send.at[z, way], code_recv.at[z],
            pb=place + (n_y if way else -n_y),
        )

    def code_hops(act):
        for way, there in ((0, hops_left), (1, hops_right)):
            @pl.when(there)
            def _():
                act(code_hop(way))

    hops(lambda item: item.start())
    for which in range(2):
        for head in (core, other):
            side_copy(which, head).start()
    for which in (0, 2, 1):
        swap(which).start()
    code_hops(lambda item: item.start())

    @pl.when(at_end)
    def _():
        for which in range(2):
            for head in (core, other):
                end_copy(which, head).start()


    def wait_kv(which, side, ka):
        target = (kbuf, vbuf)[which].at[side, rows_of(ka)]
        remote(target, target, side_send.at[which, 0], kv_recv.at[which, side, ka], ka=other).wait_recv()

    row = lax.broadcasted_iota(jnp.int32, (STATS, tile), 0)
    shards = pairs_ref.shape[3]
    def pick_of(owner):
        pick = (
            lax.broadcasted_iota(jnp.int32, (STATS, shards), 1)
            == lax.broadcasted_iota(jnp.int32, (STATS, shards), 0) // blocks + owner * n_y * n_ka
        )
        return jnp.where(pick, 1.0, 0.0).astype(jnp.bfloat16)

    mine = pick_of(z)
    wanted = lax.broadcasted_iota(jnp.int32, (STATS, tile), 1) // BLOCK * blocks + row % blocks
    wanted = wanted.astype(jnp.float32)

    def mask(layer, listed, pick, start):
        spread = lax.dot_general(
            pick, listed.astype(jnp.float32).astype(jnp.bfloat16), (((1,), (1,)), ((), ())),
            preferred_element_type=jnp.float32,
        )
        hit = None
        for slot in range(listed.shape[0]):
            same = jnp.broadcast_to(spread[:, slot : slot + 1], (STATS, tile)) == wanted
            hit = same if hit is None else hit | same
        qturned[layer, pl.ds(start, STATS), :] = jnp.where(hit, 0.0, NEGATIVE_FILL).astype(qturned.dtype)

    def prepare(layer, listed):
        mask(layer, listed, mine, HEAD)
        qturned[layer, pl.ds(0, HEAD), :] = qbuf[layer].T

    def scores_of(layer, side):
        keys = jnp.concatenate([kbuf[side], marks[0, side]], axis=1)
        return dot(keys, qturned[layer])

    def first_half(layer):
        scores = scores_of(layer, y)
        top = scores.max(0, keepdims=True)
        chances = jnp.exp2((scores - top) * EXP2_SCALE)
        peak[layer] = top
        total[layer] = chances.sum(0, keepdims=True)
        accum[layer] = dot(vturned[y], chances.astype(jnp.bfloat16))

    stat_row = lax.broadcasted_iota(jnp.int32, (STATS, BLOCK), 0)

    def put_piece(layer, ka, top, whole, mixed):
        mixed = mixed * (1.0 / whole)
        ref = osend.at[layer, ka]
        for index in range(blocks):
            ref[pl.ds(index * HEAD, HEAD), :] = mixed[:, index * BLOCK : (index + 1) * BLOCK].astype(osend.dtype)
        put_level(ref, top * EXP2_SCALE + jnp.log2(whole))

    def put(layer, top, whole, mixed):
        for ka in range(n_ka):
            span = slice(ka * rows, (ka + 1) * rows)
            put_piece(layer, ka, top[:, span], whole[:, span], mixed[:, span])

    def second_state(layer):
        scores = scores_of(layer, far_y)
        before = peak[layer]
        top = jnp.maximum(before, scores.max(0, keepdims=True))
        rescale = jnp.exp2((before - top) * EXP2_SCALE)
        chances = jnp.exp2((scores - top) * EXP2_SCALE)
        whole = total[layer] * rescale + chances.sum(0, keepdims=True)
        return top, whole, accum[layer] * rescale + dot(vturned[far_y], chances.astype(jnp.bfloat16))

    def second_half(layer):
        put(layer, *second_state(layer))

    def whole_tile(layer, keys, hints, columns_of, start=0, size=tile):
        keys = jnp.concatenate([keys[...], hints[...]], axis=2).reshape(n_y * tile, 2 * HEAD)
        scores = dot(keys, qturned[layer, :, pl.ds(start, size)])
        top = scores.max(0, keepdims=True)
        chances = jnp.exp2((scores - top) * EXP2_SCALE)
        whole = chances.sum(0, keepdims=True)
        chances = chances.astype(jnp.bfloat16)
        mixed = dot(columns_of(0), chances[:tile])
        for side in range(1, n_y):
            mixed = mixed + dot(columns_of(side), chances[side * tile : (side + 1) * tile])
        return top, whole, mixed

    def both_halves(layer):
        for ka in (core, other):
            result = whole_tile(layer, kbuf, marks.at[0], lambda side: vturned[side], pl.multiple_of(ka * rows, BLOCK), rows)
            put_piece(layer, ka, *result)
            give(layer, ka)

    def end_tile():
        top, whole, mixed = whole_tile(z, kend, marks.at[1], lambda side: vend[side].T)
        before = peak[z]
        after = jnp.maximum(before, top)
        old, new = jnp.exp2((before - after) * EXP2_SCALE), jnp.exp2((top - after) * EXP2_SCALE)
        put(z, after, total[z] * old + whole * new, accum[z] * old + mixed * new)

    def put_level(ref, level):
        high = level.astype(jnp.bfloat16).astype(jnp.float32)
        middle = (level - high).astype(jnp.bfloat16).astype(jnp.float32)
        low = level - high - middle
        stats = jnp.zeros((STATS, BLOCK), jnp.float32)
        for index in range(blocks):
            for order, term in enumerate((high, middle, low)):
                stats = jnp.where(stat_row == 3 * index + order, term[:, index * BLOCK : (index + 1) * BLOCK], stats)
        ref[pl.ds(blocks * HEAD, STATS), :] = stats.astype(ref.dtype)

    def level_of(ref):
        stats = ref[pl.ds(blocks * HEAD, STATS), :].astype(jnp.float32)
        levels = [stats[3 * i : 3 * i + 1] + stats[3 * i + 1 : 3 * i + 2] + stats[3 * i + 2 : 3 * i + 3] for i in range(blocks)]
        return jnp.concatenate(levels, axis=1)

    def blend(refs):
        levels = [level_of(ref) for ref in refs]
        top = functools.reduce(jnp.maximum, levels)
        shares = [jnp.exp2(level - top) for level in levels]
        whole = functools.reduce(jnp.add, shares)
        scale = 1.0 / whole
        shares = [share * scale for share in shares]
        mixed = []
        for index in range(blocks):
            span = slice(index * BLOCK, (index + 1) * BLOCK)
            terms = [ref[pl.ds(index * HEAD, HEAD), :].astype(jnp.float32) * share[:, span] for ref, share in zip(refs, shares)]
            mixed.append(functools.reduce(jnp.add, terms))
        return mixed, top + jnp.log2(whole)

    def merge(into, ref):
        mixed, level = blend((into, ref))
        for index in range(blocks):
            into[pl.ds(index * HEAD, HEAD), :] = mixed[index].astype(into.dtype)
        put_level(into, level)

    def straight(layer, ka):
        return remote(
            osend.at[layer, ka], orecv.at[z, core], out_send.at[layer, ka], out_recv.at[z, core],
            pb=layer * n_y + y, ka=ka,
        )

    def between(layer, ka):
        side = jnp.where(layer < z, 0, 1)
        return remote(
            osend.at[layer, ka], mrecv.at[side, ka], out_send.at[layer, ka], merge_recv.at[side, ka],
            pb=jnp.where(layer < z, place - n_y, place + n_y),
        )

    def two_away(layer):
        return jnp.logical_or(layer == z + 2, layer == z - 2)

    def is_end(layer):
        return jnp.logical_or(layer == 0, layer == n_z - 1)

    def merges(layer, ka):
        return jnp.logical_and(two_away(layer), jnp.logical_or(ka != core, jnp.logical_not(is_end(layer))))

    def give(layer, ka):
        @pl.when(merges(layer, ka))
        def _():
            between(layer, ka).start()

        @pl.when(jnp.logical_not(merges(layer, ka)))
        def _():
            straight(layer, ka).start()

    def give_other():
        return remote(
            osend.at[z, other], orecv.at[z, core], out_send.at[z, other], out_recv.at[z, core], ka=other,
        )

    shorter = jnp.minimum(z, n_z - 1 - z)
    long_right = z < n_z - 1 - z

    def layer_at(turn):
        both = turn <= 2 * shorter
        away = jnp.where(both, (turn + 1) // 2, turn - shorter)
        longer = jnp.where(both, turn % 2, 1)
        step = away * (2 * longer - 1)
        return jnp.where(long_right, z + step, z - step)

    def onward(layer):
        return jnp.logical_or(
            jnp.logical_and(layer < z, has_right), jnp.logical_and(layer > z, has_left)
        )

    def forward(layer, ka, part):
        ref = query_part(layer, ka, part)
        return remote(
            ref, ref, query_send.at[layer, ka, part], query_recv.at[layer, ka, part],
            pb=jnp.where(layer < z, place + n_y, place - n_y),
        )

    def code_forward(layer):
        return remote(
            codes.at[layer], codes.at[layer], code_send.at[layer, 0], code_recv.at[layer],
            pb=jnp.where(layer < z, place + n_y, place - n_y),
        )

    def take(layer, parts=tuple(range(cut))):
        for part in parts:
            for ka in (core, other):
                forward(layer, ka, part).wait_recv()

                @pl.when(onward(layer))
                def _():
                    forward(layer, ka, part).start()

            if part == 0:
                code_forward(layer).wait_recv()

                @pl.when(onward(layer))
                def _():
                    code_forward(layer).start()

    def ready(layer):
        prepare(layer, codes[layer, :, 0, :])

    for item in stage:
        item.wait()
    wait_kv(0, y, other)
    incoming = qbuf.at[z, other_rows]
    remote(incoming, incoming, swap_send.at[2], query_recv.at[z, other, 0], ka=other).wait_recv()
    prepare(z, pairs_ref[core, :, 0, :])
    wait_kv(1, y, other)
    vturned[y] = vbuf[y].T
    first_half(z)

    middle = jnp.logical_not(at_end)
    one, two, three = layer_at(1), layer_at(2), layer_at(3)

    @pl.when(middle)
    def _():
        take(one)
        take(two)
        ready(one)
        first_half(one)
        take(three, (0,))
        ready(two)
        first_half(two)
        take(three, tuple(range(1, cut)))
        ready(three)

    @pl.when(at_end)
    def _():
        take(two)
        ready(two)
        first_half(two)

    pass_end(0)
    for which in range(2):
        for ka in range(n_ka):
            wait_kv(which, far_y, ka)
    vturned[far_y] = vbuf[far_y].T

    def give_all(layer):
        for ka in (core, other):
            give(layer, ka)

    @pl.when(middle)
    def _():
        both_halves(three)
        second_half(two)

        @pl.when(by_end)
        def _():
            straight(two, core).start()

        second_half(one)
        pass_end(1)

        @pl.when(by_end)
        def _():
            mask(z, pairs_ref[core, :, 0, :], pick_of(last), HEAD + STATS)


    @pl.when(at_end)
    def _():
        second_half(two)
        give_all(two)
        take(three)
        ready(three)
        both_halves(three)

    late = jnp.where(at_end, three, two)

    if n_z > 4:
        def visit(turn, carry):
            layer = layer_at(turn)
            take(layer)
            ready(layer)
            both_halves(layer)
            return carry

        lax.fori_loop(4, n_z, visit, 0)

    @pl.when(jnp.logical_not(by_end))
    def _():
        second_half(z)
        give_other().start()

    @pl.when(by_end)
    def _():
        peak[z], total[z], accum[z] = second_state(z)

    @pl.when(middle)
    def _():
        for layer in (one, two):
            side = jnp.where(layer < z, 0, 1)
            for ka in range(n_ka):
                @pl.when(jnp.logical_or(ka != core, jnp.logical_not(is_end(layer))))
                def _(layer=layer, side=side, ka=ka):
                    ref = mrecv.at[side, ka]
                    remote(ref, ref, out_send.at[layer, ka], merge_recv.at[side, ka], ka=other).wait_recv()
                    merge(osend.at[layer, ka], ref)
                    straight(layer, ka).start()

    @pl.when(by_end)
    def _():
        for which in range(2):
            for ka in range(n_ka):
                wait_end(which, far_y, ka)
        end_tile()
        give_other().start()

    def wait_out(layer, head):
        ref = orecv.at[layer, head]
        remote(ref, ref, out_send.at[z, 0], out_recv.at[layer, head], ka=other).wait_recv()

    wait_out(z, other)
    if n_z > 4:
        def gather(turn, carry):
            layer = layer_at(turn)

            @pl.when(jnp.logical_not(two_away(layer)))
            def _():
                for head in (core, other):
                    wait_out(layer, head)
                merge(osend.at[z, core], orecv.at[layer, core])
                merge(orecv.at[z, other], orecv.at[layer, other])

            return carry

        lax.fori_loop(4, n_z, gather, 0)
    @pl.when(at_end)
    def _():
        wait_out(two, core)
        merge(osend.at[z, core], orecv.at[two, core])

    def keep(index, head):
        return pltpu.make_async_copy(obuf.at[index], out_ref.at[:, columns(head)], local_sem.at[3 + index])

    def conclude(sources):
        for index, head in enumerate((core, other)):
            for layer in sources:
                wait_out(layer, head)
            refs = [orecv.at[z, head] if index else osend.at[z, core]]
            refs += [orecv.at[layer, head] for layer in sources]
            for block, mixed in enumerate(blend(refs)[0]):
                obuf[index, pl.ds(block * BLOCK, BLOCK), :] = mixed.T.astype(obuf.dtype)
            keep(index, head).start()

    @pl.when(by_end)
    def _():
        conclude((one,))

    @pl.when(jnp.logical_not(by_end))
    def _():
        conclude((one, late))

    hops(lambda item: item.wait_send())
    for which in range(2):
        for head in range(n_ka):
            side_copy(which, head).wait_send()
    for which in range(3):
        swap(which).wait_send()
    code_hops(lambda item: item.wait_send())

    def drain(turn, carry):
        layer = layer_at(turn)

        @pl.when(jnp.logical_or(middle, turn != 1))
        def _():
            for ka in range(n_ka):
                straight(layer, ka).wait_send()

        @pl.when(onward(layer))
        def _():
            code_forward(layer).wait_send()
            for ka in range(n_ka):
                for part in range(cut):
                    forward(layer, ka, part).wait_send()

        return carry

    lax.fori_loop(1, n_z, drain, 0)

    @pl.when(at_end)
    def _():
        for which in range(2):
            for head in range(n_ka):
                end_copy(which, head).wait_send()

    @pl.when(by_end)
    def _():
        for which in range(2):
            for ka in range(n_ka):
                end_pass(which, ka).wait_send()

    give_other().wait_send()
    for index, head in enumerate((core, other)):
        keep(index, head).wait()


def solution(mesh):
    n_pb, n_ka = mesh.shape["pb"], mesh.shape["ka"]
    width = 2
    cut = 2

    def local(queries, keys, values, block_pairs):
        rows = queries.shape[0]
        tile = n_ka * rows
        shards, most = block_pairs.shape[2:]
        n_z = n_pb // width
        anywhere = pl.BlockSpec(memory_space=pl.ANY)
        half = jnp.bfloat16
        dma = pltpu.SemaphoreType.DMA
        return pl.pallas_call(
            functools.partial(kernel, n_pb, n_ka, width, cut),
            out_shape=jax.ShapeDtypeStruct(queries.shape, queries.dtype),
            in_specs=[anywhere, anywhere, anywhere, pl.BlockSpec(memory_space=pltpu.VMEM)],
            out_specs=anywhere,
            scratch_shapes=[
                pltpu.VMEM((n_z, tile, HEAD), half),
                pltpu.VMEM((width, tile, HEAD), half),
                pltpu.VMEM((width, tile, HEAD), half),
                pltpu.VMEM((width, tile, HEAD), half),
                pltpu.VMEM((width, tile, HEAD), half),
                pltpu.VMEM((n_z, most, 1, shards), jnp.int32),
                pltpu.VMEM((2, width, tile, HEAD), half),
                pltpu.VMEM((n_z, 2 * HEAD, tile), half),
                pltpu.VMEM((width, HEAD, tile), half),
                pltpu.VMEM((n_z, 1, tile), jnp.float32),
                pltpu.VMEM((n_z, 1, tile), jnp.float32),
                pltpu.VMEM((n_z, HEAD, tile), jnp.float32),
                pltpu.VMEM((n_z, n_ka, rows + STATS, HEAD), half),
                pltpu.VMEM((n_z, n_ka, rows + STATS, HEAD), half),
                pltpu.VMEM((2, n_ka, rows + STATS, HEAD), half),
                pltpu.VMEM((n_ka, rows, HEAD), half),
                dma((2, n_ka, cut)),
                dma((n_z, n_ka, cut)),
                dma((n_z, n_ka, cut)),
                dma((n_z, 2)),
                dma((n_z,)),
                dma((2, n_ka)),
                dma((2, width, n_ka)),
                dma((3,)),
                dma((n_z, n_ka)),
                dma((n_z, n_ka)),
                dma((2, n_ka)),
                dma((2, n_ka)),
                dma((2, width, n_ka)),
                dma((5,)),
            ],
            compiler_params=pltpu.CompilerParams(
                collective_id=0, has_side_effects=True, vmem_limit_bytes=56 * 1024 * 1024
            ),
        )(queries, keys, values, block_pairs.transpose(0, 3, 1, 2))

    rows_spec = P(("groups", "pb", "ka"), None)
    return jax.shard_map(
        local, mesh=mesh,
        in_specs=(rows_spec, rows_spec, rows_spec, P("groups", "pb", None, None)),
        out_specs=rows_spec, check_vma=False,
    )
```

```python
import functools
import math

import jax
import jax.numpy as jnp
from jax import lax
from jax.experimental import pallas as pl
from jax.experimental.pallas import tpu as pltpu
from jax.sharding import PartitionSpec as P

HEAD = 128
BLOCK = 128
STATS = 16
NEGATIVE_FILL = -1e30
EXP2_SCALE = HEAD ** (-0.5) * math.log2(math.e)
MESH = pl.DeviceIdType.MESH


def dot(a, b):
    return lax.dot_general(a, b, (((1,), (0,)), ((), ())), preferred_element_type=jnp.float32)


def kernel(
    n_pb, n_ka, width, cut, q_ref, k_ref, v_ref, pairs_ref, out_ref,
    qbuf, kbuf, vbuf, kend, vend, codes, marks, qturned, vturned, peak, total, accum, osend, orecv, mrecv, obuf,
    hop_send, query_send, query_recv, code_send, code_recv, side_send, kv_recv,
    swap_send, out_send, out_recv, merge_recv, end_send, end_recv, local_sem,
):
    rows = q_ref.shape[0]
    tile = n_ka * rows
    blocks = rows // BLOCK
    n_y = width
    n_z = n_pb // n_y
    core = lax.axis_index("ka")
    place = lax.axis_index("pb")
    z, y = place // n_y, place % n_y
    other = 1 - core
    far_y = 1 - y
    across = z * n_y + far_y
    has_left, has_right = z > 0, z < n_z - 1
    piece = rows // cut

    barrier = pltpu.get_barrier_semaphore()

    def greet(pb, ka):
        pl.semaphore_signal(barrier, inc=1, device_id={"pb": pb, "ka": ka}, device_id_type=MESH)

    at_end = jnp.logical_not(jnp.logical_and(has_left, has_right))
    by_end = jnp.logical_or(z == 1, z == n_z - 2)
    last = jnp.where(z < n_z - 1 - z, 0, n_z - 1)
    inner = jnp.where(has_left, place - n_y, place + n_y)
    hops_left, hops_right = z > 1, z < n_z - 2
    hops_left = jnp.logical_or(hops_left, z == n_z - 1)
    hops_right = jnp.logical_or(hops_right, z == 0)
    for ka in range(n_ka):
        @pl.when(has_left)
        def _():
            greet(place - n_y, ka)

        @pl.when(has_right)
        def _():
            greet(place + n_y, ka)

        greet(across, ka)
    greet(place, other)

    def columns(head):
        return pl.ds(pl.multiple_of(head * HEAD, HEAD), HEAD)

    def rows_of(ka):
        return pl.ds(pl.multiple_of(ka * rows, BLOCK), rows)

    my_rows, other_rows = rows_of(core), rows_of(other)

    stage = [
        pltpu.make_async_copy(k_ref.at[:, columns(core)], kbuf.at[y, my_rows], local_sem.at[0]),
        pltpu.make_async_copy(q_ref.at[:, columns(core)], qbuf.at[z, my_rows], local_sem.at[1]),
        pltpu.make_async_copy(v_ref.at[:, columns(core)], vbuf.at[y, my_rows], local_sem.at[2]),
    ]
    for item in stage:
        item.start()

    def remote(source, target, send_sem, recv_sem, **device):
        return pltpu.make_async_remote_copy(
            src_ref=source, dst_ref=target, send_sem=send_sem, recv_sem=recv_sem,
            device_id=device, device_id_type=MESH,
        )

    block_of_row = lax.broadcasted_iota(jnp.int32, (tile, HEAD), 0) // BLOCK
    lane = lax.broadcasted_iota(jnp.int32, (tile, HEAD), 1)
    for side in range(n_y):
        here = lane == block_of_row + side * n_ka * blocks
        marks[0, side] = jnp.where(here, 1.0, 0.0).astype(marks.dtype)
        there = lane == block_of_row + side * n_ka * blocks + STATS
        marks[1, side] = jnp.where(there, 1.0, 0.0).astype(marks.dtype)
    pad = qturned.shape[1] - HEAD - STATS
    for layer in range(n_z):
        qturned[layer, pl.ds(HEAD + STATS, pad), :] = jnp.zeros((pad, tile), qturned.dtype)

    beside = has_left.astype(jnp.int32) + has_right.astype(jnp.int32)
    pl.semaphore_wait(barrier, n_ka * (1 + beside) + 1)

    def query_part(layer, ka, part):
        return qbuf.at[layer, pl.ds(pl.multiple_of(ka * rows + part * piece, 16), piece)]

    def hop(way, head, part):
        return remote(
            q_ref.at[pl.ds(part * piece, piece), columns(head)], query_part(z, core, part),
            hop_send.at[way, head, part], query_recv.at[z, core, part],
            pb=place + (n_y if way else -n_y), ka=head,
        )

    def hops(act):
        for part in range(cut):
            for way, there in ((0, hops_left), (1, hops_right)):
                @pl.when(there)
                def _():
                    for head in (core, other):
                        act(hop(way, head, part))

    def side_copy(which, head):
        source, target = ((k_ref, kbuf), (v_ref, vbuf))[which]
        return remote(
            source.at[:, columns(head)], target.at[y, my_rows],
            side_send.at[which, head], kv_recv.at[which, y, core], pb=across, ka=head,
        )

    def end_copy(which, head):
        source, target = ((k_ref, kend), (v_ref, vend))[which]
        return remote(
            source.at[:, columns(head)], target.at[y, my_rows],
            end_send.at[which, head], end_recv.at[which, y, core], pb=inner, ka=head,
        )

    def end_pass(which, ka):
        ref = (kend, vend)[which].at[y, rows_of(ka)]
        return remote(ref, ref, end_send.at[which, ka], end_recv.at[which, y, ka], pb=across)

    def wait_end(which, side, ka):
        ref = (kend, vend)[which].at[side, rows_of(ka)]
        remote(ref, ref, end_send.at[which, ka], end_recv.at[which, side, ka], pb=across).wait_recv()

    def pass_end(which):
        @pl.when(by_end)
        def _():
            for ka in (core, other):
                wait_end(which, y, ka)
                end_pass(which, ka).start()

    def swap(which):
        source, target = (
            (k_ref, kbuf.at[y, my_rows]), (v_ref, vbuf.at[y, my_rows]), (q_ref, qbuf.at[z, my_rows]),
        )[which]
        recv = query_recv.at[z, core, 0] if which == 2 else kv_recv.at[which, y, core]
        return remote(
            source.at[:, columns(other)], target, swap_send.at[which], recv, ka=other,
        )

    def code_hop(way):
        return remote(
            pairs_ref.at[core], codes.at[z], code_send.at[z, way], code_recv.at[z],
            pb=place + (n_y if way else -n_y),
        )

    def code_hops(act):
        for way, there in ((0, hops_left), (1, hops_right)):
            @pl.when(there)
            def _():
                act(code_hop(way))

    hops(lambda item: item.start())
    for which in range(2):
        for head in (core, other):
            side_copy(which, head).start()
    for which in (0, 2, 1):
        swap(which).start()
    code_hops(lambda item: item.start())

    @pl.when(at_end)
    def _():
        for which in range(2):
            for head in (core, other):
                end_copy(which, head).start()


    def wait_kv(which, side, ka):
        target = (kbuf, vbuf)[which].at[side, rows_of(ka)]
        remote(target, target, side_send.at[which, 0], kv_recv.at[which, side, ka], ka=other).wait_recv()

    row = lax.broadcasted_iota(jnp.int32, (STATS, tile), 0)
    shards = pairs_ref.shape[3]
    def pick_of(owner):
        pick = (
            lax.broadcasted_iota(jnp.int32, (STATS, shards), 1)
            == lax.broadcasted_iota(jnp.int32, (STATS, shards), 0) // blocks + owner * n_y * n_ka
        )
        return jnp.where(pick, 1.0, 0.0).astype(jnp.bfloat16)

    mine = pick_of(z)
    wanted = lax.broadcasted_iota(jnp.int32, (STATS, tile), 1) // BLOCK * blocks + row % blocks
    wanted = wanted.astype(jnp.float32)

    def mask(layer, listed, pick, start):
        spread = lax.dot_general(
            pick, listed.astype(jnp.float32).astype(jnp.bfloat16), (((1,), (1,)), ((), ())),
            preferred_element_type=jnp.float32,
        )
        hit = None
        for slot in range(listed.shape[0]):
            same = jnp.broadcast_to(spread[:, slot : slot + 1], (STATS, tile)) == wanted
            hit = same if hit is None else hit | same
        qturned[layer, pl.ds(start, STATS), :] = jnp.where(hit, 0.0, NEGATIVE_FILL).astype(qturned.dtype)

    def prepare(layer, listed):
        mask(layer, listed, mine, HEAD)
        qturned[layer, pl.ds(0, HEAD), :] = qbuf[layer].T

    def scores_of(layer, side):
        keys = jnp.concatenate([kbuf[side], marks[0, side]], axis=1)
        return dot(keys, qturned[layer])

    def first_half(layer):
        scores = scores_of(layer, y)
        top = scores.max(0, keepdims=True)
        chances = jnp.exp2((scores - top) * EXP2_SCALE)
        peak[layer] = top
        total[layer] = chances.sum(0, keepdims=True)
        accum[layer] = dot(vturned[y], chances.astype(jnp.bfloat16))

    stat_row = lax.broadcasted_iota(jnp.int32, (STATS, BLOCK), 0)

    def put_piece(layer, ka, top, whole, mixed):
        mixed = mixed * (1.0 / whole)
        ref = osend.at[layer, ka]
        for index in range(blocks):
            ref[pl.ds(index * HEAD, HEAD), :] = mixed[:, index * BLOCK : (index + 1) * BLOCK].astype(osend.dtype)
        put_level(ref, top * EXP2_SCALE + jnp.log2(whole))

    def put(layer, top, whole, mixed):
        for ka in range(n_ka):
            span = slice(ka * rows, (ka + 1) * rows)
            put_piece(layer, ka, top[:, span], whole[:, span], mixed[:, span])

    def second_state(layer):
        scores = scores_of(layer, far_y)
        before = peak[layer]
        top = jnp.maximum(before, scores.max(0, keepdims=True))
        rescale = jnp.exp2((before - top) * EXP2_SCALE)
        chances = jnp.exp2((scores - top) * EXP2_SCALE)
        whole = total[layer] * rescale + chances.sum(0, keepdims=True)
        return top, whole, accum[layer] * rescale + dot(vturned[far_y], chances.astype(jnp.bfloat16))

    def second_half(layer):
        put(layer, *second_state(layer))

    def second_pieces(layer, act):
        keys = jnp.concatenate([kbuf[far_y], marks[0, far_y]], axis=1)
        for ka in (core, other):
            span = pl.ds(pl.multiple_of(ka * rows, BLOCK), rows)
            scores = dot(keys, qturned[layer, :, span])
            before = peak[layer, :, span]
            top = jnp.maximum(before, scores.max(0, keepdims=True))
            rescale = jnp.exp2((before - top) * EXP2_SCALE)
            chances = jnp.exp2((scores - top) * EXP2_SCALE)
            whole = total[layer, :, span] * rescale + chances.sum(0, keepdims=True)
            mixed = accum[layer, :, span] * rescale + dot(vturned[far_y], chances.astype(jnp.bfloat16))
            put_piece(layer, ka, top, whole, mixed)
            act(layer, ka)

    def whole_tile(layer, keys, hints, columns_of, start=0, size=tile):
        keys = jnp.concatenate([keys[...], hints[...]], axis=2).reshape(n_y * tile, 2 * HEAD)
        scores = dot(keys, qturned[layer, :, pl.ds(start, size)])
        top = scores.max(0, keepdims=True)
        chances = jnp.exp2((scores - top) * EXP2_SCALE)
        whole = chances.sum(0, keepdims=True)
        chances = chances.astype(jnp.bfloat16)
        mixed = dot(columns_of(0), chances[:tile])
        for side in range(1, n_y):
            mixed = mixed + dot(columns_of(side), chances[side * tile : (side + 1) * tile])
        return top, whole, mixed

    def both_halves(layer):
        for ka in (core, other):
            result = whole_tile(layer, kbuf, marks.at[0], lambda side: vturned[side], pl.multiple_of(ka * rows, BLOCK), rows)
            put_piece(layer, ka, *result)
            give(layer, ka)

    def end_tile():
        top, whole, mixed = whole_tile(z, kend, marks.at[1], lambda side: vend[side].T)
        before = peak[z]
        after = jnp.maximum(before, top)
        old, new = jnp.exp2((before - after) * EXP2_SCALE), jnp.exp2((top - after) * EXP2_SCALE)
        put(z, after, total[z] * old + whole * new, accum[z] * old + mixed * new)

    def put_level(ref, level):
        high = level.astype(jnp.bfloat16).astype(jnp.float32)
        middle = (level - high).astype(jnp.bfloat16).astype(jnp.float32)
        low = level - high - middle
        stats = jnp.zeros((STATS, BLOCK), jnp.float32)
        for index in range(blocks):
            for order, term in enumerate((high, middle, low)):
                stats = jnp.where(stat_row == 3 * index + order, term[:, index * BLOCK : (index + 1) * BLOCK], stats)
        ref[pl.ds(blocks * HEAD, STATS), :] = stats.astype(ref.dtype)

    def level_of(ref):
        stats = ref[pl.ds(blocks * HEAD, STATS), :].astype(jnp.float32)
        levels = [stats[3 * i : 3 * i + 1] + stats[3 * i + 1 : 3 * i + 2] + stats[3 * i + 2 : 3 * i + 3] for i in range(blocks)]
        return jnp.concatenate(levels, axis=1)

    def blend(refs):
        levels = [level_of(ref) for ref in refs]
        top = functools.reduce(jnp.maximum, levels)
        shares = [jnp.exp2(level - top) for level in levels]
        whole = functools.reduce(jnp.add, shares)
        scale = 1.0 / whole
        shares = [share * scale for share in shares]
        mixed = []
        for index in range(blocks):
            span = slice(index * BLOCK, (index + 1) * BLOCK)
            terms = [ref[pl.ds(index * HEAD, HEAD), :].astype(jnp.float32) * share[:, span] for ref, share in zip(refs, shares)]
            mixed.append(functools.reduce(jnp.add, terms))
        return mixed, top + jnp.log2(whole)

    def merge(into, ref):
        mixed, level = blend((into, ref))
        for index in range(blocks):
            into[pl.ds(index * HEAD, HEAD), :] = mixed[index].astype(into.dtype)
        put_level(into, level)

    def straight(layer, ka):
        return remote(
            osend.at[layer, ka], orecv.at[z, core], out_send.at[layer, ka], out_recv.at[z, core],
            pb=layer * n_y + y, ka=ka,
        )

    def between(layer, ka):
        side = jnp.where(layer < z, 0, 1)
        return remote(
            osend.at[layer, ka], mrecv.at[side, ka], out_send.at[layer, ka], merge_recv.at[side, ka],
            pb=jnp.where(layer < z, place - n_y, place + n_y),
        )

    def two_away(layer):
        return jnp.logical_or(layer == z + 2, layer == z - 2)

    def is_end(layer):
        return jnp.logical_or(layer == 0, layer == n_z - 1)

    def merges(layer, ka):
        return jnp.logical_and(two_away(layer), jnp.logical_or(ka != core, jnp.logical_not(is_end(layer))))

    def give(layer, ka):
        @pl.when(merges(layer, ka))
        def _():
            between(layer, ka).start()

        @pl.when(jnp.logical_not(merges(layer, ka)))
        def _():
            straight(layer, ka).start()

    def give_other():
        return remote(
            osend.at[z, other], orecv.at[z, core], out_send.at[z, other], out_recv.at[z, core], ka=other,
        )

    shorter = jnp.minimum(z, n_z - 1 - z)
    long_right = z < n_z - 1 - z

    def layer_at(turn):
        both = turn <= 2 * shorter
        away = jnp.where(both, (turn + 1) // 2, turn - shorter)
        longer = jnp.where(both, turn % 2, 1)
        step = away * (2 * longer - 1)
        return jnp.where(long_right, z + step, z - step)

    def onward(layer):
        return jnp.logical_or(
            jnp.logical_and(layer < z, has_right), jnp.logical_and(layer > z, has_left)
        )

    def forward(layer, ka, part):
        ref = query_part(layer, ka, part)
        return remote(
            ref, ref, query_send.at[layer, ka, part], query_recv.at[layer, ka, part],
            pb=jnp.where(layer < z, place + n_y, place - n_y),
        )

    def code_forward(layer):
        return remote(
            codes.at[layer], codes.at[layer], code_send.at[layer, 0], code_recv.at[layer],
            pb=jnp.where(layer < z, place + n_y, place - n_y),
        )

    def take(layer, parts=tuple(range(cut))):
        for part in parts:
            for ka in (core, other):
                forward(layer, ka, part).wait_recv()

                @pl.when(onward(layer))
                def _():
                    forward(layer, ka, part).start()

            if part == 0:
                code_forward(layer).wait_recv()

                @pl.when(onward(layer))
                def _():
                    code_forward(layer).start()

    def ready(layer):
        prepare(layer, codes[layer, :, 0, :])

    for item in stage:
        item.wait()
    wait_kv(0, y, other)
    incoming = qbuf.at[z, other_rows]
    remote(incoming, incoming, swap_send.at[2], query_recv.at[z, other, 0], ka=other).wait_recv()
    prepare(z, pairs_ref[core, :, 0, :])
    wait_kv(1, y, other)
    vturned[y] = vbuf[y].T
    first_half(z)

    middle = jnp.logical_not(at_end)
    one, two, three = layer_at(1), layer_at(2), layer_at(3)

    @pl.when(middle)
    def _():
        take(one)
        take(two)
        ready(one)
        first_half(one)
        take(three, (0,))
        ready(two)
        first_half(two)
        take(three, tuple(range(1, cut)))
        ready(three)

    @pl.when(at_end)
    def _():
        take(two)
        ready(two)
        first_half(two)

    pass_end(0)
    for which in range(2):
        for ka in range(n_ka):
            wait_kv(which, far_y, ka)
    vturned[far_y] = vbuf[far_y].T

    @pl.when(middle)
    def _():
        both_halves(three)
        def forth(layer, ka):
            if ka is core:
                @pl.when(by_end)
                def _():
                    straight(layer, ka).start()

        second_pieces(two, forth)

        second_half(one)
        pass_end(1)

        @pl.when(by_end)
        def _():
            mask(z, pairs_ref[core, :, 0, :], pick_of(last), HEAD + STATS)


    @pl.when(at_end)
    def _():
        second_pieces(two, give)
        take(three)
        ready(three)
        both_halves(three)

    late = jnp.where(at_end, three, two)

    if n_z > 4:
        def visit(turn, carry):
            layer = layer_at(turn)
            take(layer)
            ready(layer)
            both_halves(layer)
            return carry

        lax.fori_loop(4, n_z, visit, 0)

    @pl.when(jnp.logical_not(by_end))
    def _():
        second_half(z)
        give_other().start()

    @pl.when(by_end)
    def _():
        peak[z], total[z], accum[z] = second_state(z)

    @pl.when(middle)
    def _():
        for layer in (one, two):
            side = jnp.where(layer < z, 0, 1)
            for ka in range(n_ka):
                @pl.when(jnp.logical_or(ka != core, jnp.logical_not(is_end(layer))))
                def _(layer=layer, side=side, ka=ka):
                    ref = mrecv.at[side, ka]
                    remote(ref, ref, out_send.at[layer, ka], merge_recv.at[side, ka], ka=other).wait_recv()
                    merge(osend.at[layer, ka], ref)
                    straight(layer, ka).start()

    @pl.when(by_end)
    def _():
        for which in range(2):
            for ka in range(n_ka):
                wait_end(which, far_y, ka)
        end_tile()
        give_other().start()

    def wait_out(layer, head):
        ref = orecv.at[layer, head]
        remote(ref, ref, out_send.at[z, 0], out_recv.at[layer, head], ka=other).wait_recv()

    wait_out(z, other)
    if n_z > 4:
        def gather(turn, carry):
            layer = layer_at(turn)

            @pl.when(jnp.logical_not(two_away(layer)))
            def _():
                for head in (core, other):
                    wait_out(layer, head)
                merge(osend.at[z, core], orecv.at[layer, core])
                merge(orecv.at[z, other], orecv.at[layer, other])

            return carry

        lax.fori_loop(4, n_z, gather, 0)
    @pl.when(at_end)
    def _():
        wait_out(two, core)
        merge(osend.at[z, core], orecv.at[two, core])

    def keep(index, head):
        return pltpu.make_async_copy(obuf.at[index], out_ref.at[:, columns(head)], local_sem.at[3 + index])

    def conclude(sources):
        for index, head in enumerate((core, other)):
            for layer in sources:
                wait_out(layer, head)
            refs = [orecv.at[z, head] if index else osend.at[z, core]]
            refs += [orecv.at[layer, head] for layer in sources]
            for block, mixed in enumerate(blend(refs)[0]):
                obuf[index, pl.ds(block * BLOCK, BLOCK), :] = mixed.T.astype(obuf.dtype)
            keep(index, head).start()

    @pl.when(by_end)
    def _():
        conclude((one,))

    @pl.when(jnp.logical_not(by_end))
    def _():
        conclude((one, late))

    hops(lambda item: item.wait_send())
    for which in range(2):
        for head in range(n_ka):
            side_copy(which, head).wait_send()
    for which in range(3):
        swap(which).wait_send()
    code_hops(lambda item: item.wait_send())

    def drain(turn, carry):
        layer = layer_at(turn)

        @pl.when(jnp.logical_or(middle, turn != 1))
        def _():
            for ka in range(n_ka):
                straight(layer, ka).wait_send()

        @pl.when(onward(layer))
        def _():
            code_forward(layer).wait_send()
            for ka in range(n_ka):
                for part in range(cut):
                    forward(layer, ka, part).wait_send()

        return carry

    lax.fori_loop(1, n_z, drain, 0)

    @pl.when(at_end)
    def _():
        for which in range(2):
            for head in range(n_ka):
                end_copy(which, head).wait_send()

    @pl.when(by_end)
    def _():
        for which in range(2):
            for ka in range(n_ka):
                end_pass(which, ka).wait_send()

    give_other().wait_send()
    for index, head in enumerate((core, other)):
        keep(index, head).wait()


def solution(mesh):
    n_pb, n_ka = mesh.shape["pb"], mesh.shape["ka"]
    width = 2
    cut = 2

    def local(queries, keys, values, block_pairs):
        rows = queries.shape[0]
        tile = n_ka * rows
        shards, most = block_pairs.shape[2:]
        n_z = n_pb // width
        anywhere = pl.BlockSpec(memory_space=pl.ANY)
        half = jnp.bfloat16
        dma = pltpu.SemaphoreType.DMA
        return pl.pallas_call(
            functools.partial(kernel, n_pb, n_ka, width, cut),
            out_shape=jax.ShapeDtypeStruct(queries.shape, queries.dtype),
            in_specs=[anywhere, anywhere, anywhere, pl.BlockSpec(memory_space=pltpu.VMEM)],
            out_specs=anywhere,
            scratch_shapes=[
                pltpu.VMEM((n_z, tile, HEAD), half),
                pltpu.VMEM((width, tile, HEAD), half),
                pltpu.VMEM((width, tile, HEAD), half),
                pltpu.VMEM((width, tile, HEAD), half),
                pltpu.VMEM((width, tile, HEAD), half),
                pltpu.VMEM((n_z, most, 1, shards), jnp.int32),
                pltpu.VMEM((2, width, tile, HEAD), half),
                pltpu.VMEM((n_z, 2 * HEAD, tile), half),
                pltpu.VMEM((width, HEAD, tile), half),
                pltpu.VMEM((n_z, 1, tile), jnp.float32),
                pltpu.VMEM((n_z, 1, tile), jnp.float32),
                pltpu.VMEM((n_z, HEAD, tile), jnp.float32),
                pltpu.VMEM((n_z, n_ka, rows + STATS, HEAD), half),
                pltpu.VMEM((n_z, n_ka, rows + STATS, HEAD), half),
                pltpu.VMEM((2, n_ka, rows + STATS, HEAD), half),
                pltpu.VMEM((n_ka, rows, HEAD), half),
                dma((2, n_ka, cut)),
                dma((n_z, n_ka, cut)),
                dma((n_z, n_ka, cut)),
                dma((n_z, 2)),
                dma((n_z,)),
                dma((2, n_ka)),
                dma((2, width, n_ka)),
                dma((3,)),
                dma((n_z, n_ka)),
                dma((n_z, n_ka)),
                dma((2, n_ka)),
                dma((2, n_ka)),
                dma((2, width, n_ka)),
                dma((5,)),
            ],
            compiler_params=pltpu.CompilerParams(
                collective_id=0, has_side_effects=True, vmem_limit_bytes=56 * 1024 * 1024
            ),
        )(queries, keys, values, block_pairs.transpose(0, 3, 1, 2))

    rows_spec = P(("groups", "pb", "ka"), None)
    return jax.shard_map(
        local, mesh=mesh,
        in_specs=(rows_spec, rows_spec, rows_spec, P("groups", "pb", None, None)),
        out_specs=rows_spec, check_vma=False,
    )
```
